32 devices in a mesh: tile: 16 (over z, y, core), band: 2 (over x).
Axes of the slice: x: 2, y: 2, z: 4, core: 2. Of those that a mesh axis runs over, the one named last changes fastest.
Arguments:
- stamps: bfloat16 [4096, 64, 128], P(('band', 'tile')), parts along dimension 0, may hold values from -6 to 6
- tile_of: int32 [4096, 1], P(('band', 'tile')), parts along dimension 0, may hold values from 0 to 15; in each aligned block of 128 rows (0 to 127, 128 to 255, ...) at most 10 rows name the same one
- row_offset: int32 [4096], P(('band', 'tile')), parts along dimension 0, may hold values from 0 to 7
- col_offset: int32 [4096], P(('band', 'tile')), parts along dimension 0, may hold values from 0 to 3
- psf_model: int32 [4096], P(('band', 'tile')), parts along dimension 0, may hold values from 0 to 17
- psf_rows: float32 [36, 3, 15], P('band'), parts along dimension 0, may hold values from -1.5 to 1.5
- psf_cols: float32 [36, 3, 15], P('band'), parts along dimension 0, may hold values from -1.5 to 1.5
- cotangent: bfloat16 [8192, 512], P(('band', 'tile')), parts along dimension 0, may hold values from -6 to 6
Outputs:
- tile_image: bfloat16 [8192, 512], P(('band', 'tile')), parts along dimension 0
- stamp_grad: bfloat16 [4096, 64, 128], P(('band', 'tile')), parts along dimension 0
The draws below stay inside these ranges and needn't reach their ends.
There are 2 independent parts, one for each index of `band`. The reference program is written for one: setup_inputs(seed, part) draws one part's arguments, and reference() takes and returns one part's arrays. A program takes and returns all parts, laid end to end along the dimension named above; each array names one. Nothing has to cross between parts.
Inputs may be any that keep to these rules, and one draw needn't show every extreme that they name: `tile_of`: at most 10 of the stamps of one device lie on one tile, and in every draw some device places exactly 10 stamps on some tile.
All inputs are finite; a program needn't handle non-finite values.
Results may differ from the reference program's by a relative error of at most 0.007.
Values may be sent and summed in bfloat16 or wider, within the bound.
A program may use at most 128 MiB of HBM per device.

```python
import math
import jax
import jax.numpy as jnp
import numpy as np
from jax import lax

SY = 64
SX = 128
KW = 15
TERMS = 3
NPSF = 18
STAMPS = 128
TY = 256
TX = 512
BY = 32
NTILES = 16
STAMPS_ALL = 2048
SKY = 4096
CAP = 10


def touch_ends(drawn, stream_key, low, largest):
    longest = drawn.shape.index(max(drawn.shape))
    spots = []
    for shift in (0, 1):
        where = [jax.random.randint(jax.random.fold_in(stream_key, axis), (), 0, length) for axis, length in enumerate(drawn.shape)]
        where[longest] = (where[longest] + shift) % drawn.shape[longest]
        spots.append(tuple(where))
    return drawn.at[spots[0]].set(low).at[spots[1]].set(largest)


def steps_of(own_key, extent, shards, low, largest):
    def one(dim, shards_of):
        steps = jax.random.uniform(jax.random.fold_in(jax.random.fold_in(own_key, 6), dim), (shards_of,), jnp.float32, low / len(shards), largest / len(shards))
        return jnp.repeat(jnp.exp(steps), extent[dim] // shards_of).reshape((-1,) + (1,) * (len(extent) - dim - 1))

    factor_of = one(*shards[0])
    for cut in shards[1:]:
        factor_of = factor_of * one(*cut)
    return factor_of


def shared_out(key, own, number, rows, number_of, top, limit, skew):
    order = jax.random.permutation(key, number_of)
    packed, ordinary = load_shares(number_of, rows * top, limit, skew, True), load_shares(number_of, rows * top, limit, skew, False)
    places = jnp.arange(number_of)

    def named(tallies, rotation):
        used = int((tallies > 0).sum())
        fixed = max(1, used // 4)
        shifted = fixed + (places - fixed + rotation * (used - fixed)) % max(1, number_of - fixed)
        return jnp.zeros((number_of,), jnp.int32).at[order[jnp.where(places < fixed, places, shifted)]].set(jnp.asarray(tallies, jnp.int32))

    tallies = jnp.where(number % 4 == 0, named(packed, number // 4), named(ordinary, number - number // 4 - 1))
    mixed = jax.random.permutation(jax.random.fold_in(own, 3), number_of)
    source_of, sink = mixed[0:number_of // 2 * 2:2], mixed[1:number_of // 2 * 2:2]
    room = jnp.minimum(tallies[source_of] - 1, limit - tallies[sink]) // 2
    room = jnp.where((source_of == order[0]) | (sink == order[0]) | (tallies[sink] == 0), 0, jnp.maximum(room, 0))
    shifted = jax.random.randint(jax.random.fold_in(own, 4), (number_of // 2,), 0, 1 << 20) % (room + 1)
    tallies = tallies.at[source_of].add(-shifted).at[sink].add(shifted)
    members = jnp.searchsorted(jnp.cumsum(tallies), jnp.arange(rows * top), side="right").astype(jnp.int32)
    grid = members.reshape(top, rows).T
    grid = grid[jax.random.permutation(jax.random.fold_in(own, 1), rows)]
    rotation = jax.random.randint(jax.random.fold_in(own, 2), (rows, 1), 0, top)
    return jnp.take_along_axis(grid, (jnp.arange(top)[None, :] + rotation) % top, axis=1)


def load_shares(amount, total, reach, skew, full):
    loads = [(1 << 20) // math.isqrt(standing ** skew) + 1 for standing in range(1, amount + 1)]
    largest = reach if full else min(reach, max(-(-total // amount), total * loads[0] // sum(loads)))
    least = 1 if total - largest >= amount - 1 else 0
    holding, rest = [largest] + [least] * (amount - 1), total - largest - least * (amount - 1)
    while rest > 0:
        movable = [i for i in range(1, amount) if holding[i] < largest] or [i for i in range(1, amount) if holding[i] < reach]
        whole, budget = sum([loads[i] for i in movable]), rest
        for i in movable:
            extra = min(reach - holding[i], max(1, budget * loads[i] // whole), rest)
            holding[i] = holding[i] + extra
            rest = rest - extra
    return np.array(holding)


def normal_values(stream_key, dims, spread, reach, cuts=(), kind=jnp.bfloat16):
    array = spread * jax.random.normal(stream_key, dims, jnp.float32)
    if cuts:
        array = array * steps_of(stream_key, dims, cuts, -0.22, 0.18)
    return jnp.clip(array, -reach, reach).astype(kind)


def setup_inputs(seed: int = 0, part: int = 0) -> dict:
    arg_keys = jax.random.split(jax.random.key(seed), 9)
    part_keys = jax.random.split(jax.random.fold_in(arg_keys[8], part), 9)
    stamps = normal_values(part_keys[0], (STAMPS_ALL, SY, SX), 1.0, 6.0, ((0, 16),))
    tile_of_keys = jax.random.split(jax.random.fold_in(part_keys[1], 1), STAMPS_ALL // STAMPS)
    tile_of_turns = jax.random.permutation(jax.random.fold_in(part_keys[1], 3), STAMPS_ALL // STAMPS)
    tile_of = jax.vmap(lambda own, number: shared_out(jax.random.fold_in(part_keys[1], 2), own, number, STAMPS, NTILES, 1, CAP, 1))(tile_of_keys, tile_of_turns).reshape((STAMPS_ALL, 1))
    row_offset = touch_ends(jax.random.randint(part_keys[2], (STAMPS_ALL,), 0, TY // BY), jax.random.fold_in(part_keys[2], 1), 0, (TY // BY) - 1).astype(jnp.int32)
    col_offset = touch_ends(jax.random.randint(part_keys[3], (STAMPS_ALL,), 0, TX // SX), jax.random.fold_in(part_keys[3], 1), 0, (TX // SX) - 1).astype(jnp.int32)
    psf_model = touch_ends(jax.random.randint(part_keys[4], (STAMPS_ALL,), 0, NPSF), jax.random.fold_in(part_keys[4], 1), 0, NPSF - 1).astype(jnp.int32)
    psf_rows = normal_values(part_keys[5], (NPSF, TERMS, KW), KW ** -0.5, 1.5, (), jnp.float32)
    psf_cols = normal_values(part_keys[6], (NPSF, TERMS, KW), KW ** -0.5, 1.5, (), jnp.float32)
    cotangent = normal_values(part_keys[7], (SKY, TX), 1.0, 6.0, ((0, 16),))
    return dict(stamps=stamps, tile_of=tile_of, row_offset=row_offset, col_offset=col_offset, psf_model=psf_model, psf_rows=psf_rows, psf_cols=psf_cols, cotangent=cotangent)


def operators(profiles, size):
    half_width = (KW - 1) // 2
    places = jnp.arange(size, dtype=jnp.int32)
    offsets = places[None, :] - places[:, None] + half_width
    inside = (offsets >= 0) & (offsets < KW)
    tap_values = jnp.take(profiles, jnp.clip(offsets, 0, KW - 1), axis=2)
    return jnp.where(inside, tap_values, jnp.zeros_like(tap_values)).astype(jnp.bfloat16)


def convolve_block(images, models, row_ops, col_ops):
    row_mats = row_ops[models].astype(jnp.float32)
    col_mats = col_ops[models].astype(jnp.float32)
    row_pass = jnp.einsum("bkij,bjx->bkix", row_mats, images.astype(jnp.float32)).astype(jnp.bfloat16)
    return jnp.einsum("bkix,bkyx->biy", row_pass.astype(jnp.float32), col_mats).astype(jnp.bfloat16)


def transpose_block(windows, models, row_ops, col_ops):
    row_mats = row_ops[models].astype(jnp.float32)
    col_mats = col_ops[models].astype(jnp.float32)
    back_pass = jnp.einsum("biy,bkyx->bkix", windows.astype(jnp.float32), col_mats).astype(jnp.bfloat16)
    return jnp.einsum("bkji,bkjx->bix", row_mats, back_pass.astype(jnp.float32)).astype(jnp.bfloat16)


def reference(stamps, tile_of, row_offset, col_offset, psf_model, psf_rows, psf_cols, cotangent):
    row_ops = operators(psf_rows, SY)
    col_ops = operators(psf_cols, SX)
    grouped_models = psf_model.reshape(NTILES, STAMPS)

    def forward_group(inputs):
        return convolve_block(inputs[0], inputs[1], row_ops, col_ops)

    convolved = lax.map(forward_group, (stamps.reshape(NTILES, STAMPS, SY, SX), grouped_models))
    convolved = convolved.reshape(STAMPS_ALL, SY, SX)
    row_blocks = TY // BY
    col_blocks = TX // SX
    upper_block = tile_of[:, 0] * row_blocks + row_offset
    block_ids = (jnp.stack([upper_block, upper_block + 1], axis=1) * col_blocks + col_offset[:, None]).astype(jnp.int32)
    block_count = (NTILES * row_blocks + 1) * col_blocks
    pieces = convolved.reshape(STAMPS_ALL * 2, BY * SX).astype(jnp.float32)
    summed = jax.ops.segment_sum(pieces, block_ids.reshape(-1), num_segments=block_count)
    sky_rows = summed.reshape(NTILES * row_blocks + 1, col_blocks, BY, SX).transpose(0, 2, 1, 3)
    sky_rows = sky_rows.reshape((NTILES * row_blocks + 1) * BY, TX)
    tile_image = sky_rows[: NTILES * TY].astype(jnp.bfloat16)
    padded = jnp.concatenate([cotangent, jnp.zeros((BY, TX), cotangent.dtype)], axis=0)
    blocks = padded.reshape(NTILES * row_blocks + 1, BY, col_blocks, SX).transpose(0, 2, 1, 3)
    blocks = blocks.reshape(block_count, BY * SX)
    windows = blocks[block_ids.reshape(-1)].reshape(NTILES, STAMPS, SY, SX)

    def backward_group(inputs):
        return transpose_block(inputs[0], inputs[1], row_ops, col_ops)

    gradients = lax.map(backward_group, (windows, grouped_models)).reshape(STAMPS_ALL, SY, SX)
    return tile_image, gradients
```

```python
from functools import partial

import jax
import jax.numpy as jnp
from jax import lax
from jax.experimental import pallas as pl
from jax.experimental.pallas import tpu as pltpu
from jax.sharding import PartitionSpec as P


def passed_along(array, axis, by):
    peers = lax.axis_size(axis)
    pairs = [(i, i + by) for i in range(peers) if 0 <= i + by < peers]
    return lax.ppermute(array, axis, pairs)


def for_sending(array):

    def short(part):
        return part.astype(jnp.bfloat16) if part.dtype == jnp.float32 else part

    return jax.tree.map(short, array)


def band_table(taps_count, size):
    half_width = (taps_count - 1) // 2
    places = jnp.arange(size, dtype=jnp.int32)
    offsets = places[None, :] - places[:, None] + half_width
    taps_index = jnp.arange(taps_count, dtype=jnp.int32)
    table = (offsets[None, :, :] == taps_index[:, None, None]).astype(jnp.float32)
    return table.reshape((taps_count, size * size))


def build_ops(profiles, size):
    model_total, term_total, taps_count = profiles.shape
    table = band_table(taps_count, size)
    mats = jnp.dot(
        profiles.reshape((model_total * term_total, taps_count)),
        table,
        precision=lax.Precision.HIGHEST,
    )
    return mats.reshape((model_total, term_total, size, size)).astype(jnp.bfloat16)


def convolve_one(inputs, row_ops, col_ops):
    image, model = inputs
    row_mats = lax.dynamic_index_in_dim(row_ops, model, 0, keepdims=False)
    col_mats = lax.dynamic_index_in_dim(col_ops, model, 0, keepdims=False)
    row_pass = jnp.einsum(
        "kij,jx->kix", row_mats, image, preferred_element_type=jnp.float32
    ).astype(jnp.bfloat16)
    return jnp.einsum("kix,kyx->iy", row_pass, col_mats, preferred_element_type=jnp.float32).astype(
        jnp.bfloat16
    )


def transpose_one(inputs, row_ops, col_ops):
    window, model = inputs
    row_mats = lax.dynamic_index_in_dim(row_ops, model, 0, keepdims=False)
    col_mats = lax.dynamic_index_in_dim(col_ops, model, 0, keepdims=False)
    back_pass = jnp.einsum(
        "iy,kyx->kix", window, col_mats, preferred_element_type=jnp.float32
    ).astype(jnp.bfloat16)
    return jnp.einsum(
        "kji,kjx->ix", row_mats, back_pass, preferred_element_type=jnp.float32
    ).astype(jnp.bfloat16)


def apply_all(function, images, models, row_ops, col_ops):
    bound = partial(function, row_ops=row_ops, col_ops=col_ops)
    return lax.map(bound, (images, models.astype(jnp.int32)), batch_size=32)


def per_device(stamps, tile_of, row_offset, col_offset, psf_model, psf_rows, psf_cols, cotangent):
    peer_count = lax.axis_size("tile")
    stamp_count, stamp_rows, stamp_cols = stamps.shape
    block_rows = stamp_rows // 2
    tile_rows, tile_cols = cotangent.shape
    row_blocks = tile_rows // block_rows
    col_blocks = tile_cols // stamp_cols
    capacity = max(2, (5 * stamp_count + 4 * peer_count - 1) // (4 * peer_count))
    slot_total = peer_count * capacity
    row_ops = build_ops(psf_rows, stamp_rows)
    col_ops = build_ops(psf_cols, stamp_cols)
    target = tile_of[:, 0]
    order = jnp.arange(stamp_count, dtype=jnp.int32)
    earlier = (target[None, :] == target[:, None]) & (order[None, :] < order[:, None])
    slots = target * capacity + jnp.sum(earlier.astype(jnp.int32), axis=1)
    slot_ids = jnp.arange(slot_total, dtype=jnp.int32)
    matches = slots[None, :] == slot_ids[:, None]
    place = matches.astype(jnp.bfloat16)
    details = jnp.stack([jnp.ones_like(target), row_offset, col_offset, psf_model], axis=1)
    detail_send = jnp.sum(jnp.where(matches[:, :, None], details[None, :, :], 0), axis=1)
    detail_send = detail_send.reshape(peer_count, capacity, 4)
    raw_send = jnp.dot(
        place,
        stamps.reshape((stamp_count, stamp_rows * stamp_cols)),
        preferred_element_type=jnp.float32,
    )
    raw_send = raw_send.astype(jnp.bfloat16).reshape(peer_count, capacity, stamp_rows, stamp_cols)
    raw_part = lax.all_to_all(raw_send, "tile", split_axis=0, concat_axis=0, tiled=True)
    info_part = lax.all_to_all(detail_send, "tile", split_axis=0, concat_axis=0, tiled=True)
    flat = raw_part.reshape((-1, stamp_rows, stamp_cols))
    result = apply_all(convolve_one, flat, info_part.reshape((-1, 4))[:, 3], row_ops, col_ops)
    received = result.reshape(raw_part.shape)
    info_flat = info_part.reshape((slot_total, 4))
    upper_block = info_flat[:, 1]
    block_ids = jnp.stack([upper_block, upper_block + 1], axis=1) * col_blocks + info_flat[:, 2:3]
    targets = jnp.arange((row_blocks + 1) * col_blocks, dtype=jnp.int32)
    placing = (block_ids.reshape(-1)[None, :] == targets[:, None]).astype(jnp.bfloat16)
    pieces = received.reshape((slot_total * 2, block_rows * stamp_cols))
    extended = jnp.dot(placing, pieces, preferred_element_type=jnp.float32)
    extended = extended.reshape(row_blocks + 1, col_blocks, block_rows, stamp_cols).transpose(
        0, 2, 1, 3
    )
    extended = extended.reshape((row_blocks + 1) * block_rows, tile_cols)
    arriving = passed_along(extended[tile_rows:].astype(jnp.bfloat16), "tile", 1).astype(
        jnp.float32
    )
    tile_sum = extended[:tile_rows].at[:block_rows].add(arriving)
    tile_image = tile_sum.astype(jnp.bfloat16)
    rim = passed_along(cotangent[:block_rows], "tile", -1)
    padded = jnp.concatenate([cotangent, rim], axis=0)
    blocks = padded.reshape(row_blocks + 1, block_rows, col_blocks, stamp_cols).transpose(
        0, 2, 1, 3
    )
    blocks = blocks.reshape((row_blocks + 1) * col_blocks, block_rows * stamp_cols)
    windows = lax.dot_general(
        placing, blocks, (((0,), (0,)), ((), ())), preferred_element_type=jnp.float32
    )
    windows = windows.astype(jnp.bfloat16).reshape(slot_total, stamp_rows, stamp_cols)
    slot_grads = apply_all(transpose_one, windows, info_flat[:, 3], row_ops, col_ops)
    slot_grads = slot_grads.reshape(peer_count, capacity, stamp_rows, stamp_cols)
    returned = lax.all_to_all(
        for_sending(slot_grads), "tile", split_axis=0, concat_axis=0, tiled=True
    ).astype(slot_grads.dtype)
    stamp_grad = lax.dot_general(
        place,
        returned.reshape((slot_total, stamp_rows * stamp_cols)),
        (((0,), (0,)), ((), ())),
        preferred_element_type=jnp.float32,
    )
    stamp_grad = stamp_grad.astype(jnp.bfloat16).reshape(stamp_count, stamp_rows, stamp_cols)
    return (tile_image, stamp_grad)


def tap_rows(profiles, lanes, flip):
    models, terms, count = profiles.shape
    half = (count - 1) // 2
    flat = profiles.reshape((models * terms, count))
    if flip:
        flat = flat[:, ::-1]
    gap = jnp.zeros((models * terms, lanes - count), flat.dtype)
    return jnp.concatenate([flat[:, half:], gap, flat[:, :half]], axis=1)


def band_matrix(row, size, half):
    lanes = row.shape[-1]
    spread = jnp.broadcast_to(row, (size, lanes))
    turned = pltpu.roll(spread, 0, 1, stride=1, stride_axis=0)
    down = lax.broadcasted_iota(jnp.int32, (size, lanes), 0)
    across = lax.broadcasted_iota(jnp.int32, (size, lanes), 1)
    return jnp.where(jnp.abs(across - down) <= half, turned, 0.0).astype(jnp.bfloat16)


def forward_kernel(half, terms, model_bits, col_blocks, group, codes, rows_ref, cols_ref, stamps_ref,
                   strip_ref, row_ops, col_ops, total):
    step = pl.program_id(0)
    models, stacked, stamp_rows = row_ops.shape
    stamp_cols = col_ops.shape[2]
    block_rows = stamp_rows // 2
    strip_rows = strip_ref.shape[0]

    @pl.when(step == 0)
    def _():
        def build(m, carry):
            for k in range(terms):
                line = m * terms + k
                mat = band_matrix(rows_ref[pl.ds(line, 1), :], stamp_rows, half)
                row_ops[m, k * stamp_rows:(k + 1) * stamp_rows, :] = mat[:, :stamp_rows]
                col_ops[m, k * stamp_cols:(k + 1) * stamp_cols, :] = band_matrix(
                    cols_ref[pl.ds(line, 1), :], stamp_cols, half)
            return carry

        lax.fori_loop(0, models, build, 0)

        def clear(i, carry):
            total[pl.ds(pl.multiple_of(i * block_rows, block_rows), block_rows), :] = jnp.zeros(
                (block_rows, total.shape[1]), jnp.float32)
            return carry

        lax.fori_loop(0, total.shape[0] // block_rows, clear, 0)

    per_step = stamps_ref.shape[0]

    def some(g, carry):
        done = []
        for u in range(group):
            local = g * group + u
            code = codes[step * per_step + local]
            model = code & ((1 << model_bits) - 1)
            block = code >> model_bits
            first = jnp.dot(row_ops[model], stamps_ref[local],
                            preferred_element_type=jnp.float32).astype(jnp.bfloat16)
            wide = jnp.concatenate(
                [first[k * stamp_rows:(k + 1) * stamp_rows] for k in range(terms)], axis=1)
            out = jnp.dot(wide, col_ops[model], preferred_element_type=jnp.float32)
            done.append((block, out.astype(jnp.bfloat16).astype(jnp.float32)))
        for block, out in done:
            top = pl.multiple_of((block // col_blocks) * block_rows, block_rows)
            left = pl.multiple_of((block % col_blocks) * stamp_cols, stamp_cols)
            spot = (pl.ds(top, stamp_rows), pl.ds(left, stamp_cols))
            total[spot] = total[spot] + out
        return carry

    lax.fori_loop(0, per_step // group, some, 0)

    @pl.when(step == pl.num_programs(0) - 1)
    def _():
        def put(i, carry):
            spot = pl.ds(pl.multiple_of(i * block_rows, block_rows), block_rows)
            strip_ref[spot, :] = total[spot, :].astype(jnp.bfloat16)
            return carry

        lax.fori_loop(0, strip_rows // block_rows, put, 0)


def backward_kernel(half, terms, model_bits, col_blocks, group, codes, rows_ref, cols_ref, sky_ref,
                    grads_ref, row_ops, col_ops, sky, sem):
    step = pl.program_id(0)
    models, stamp_rows, stacked = row_ops.shape
    stamp_cols = col_ops.shape[1]
    block_rows = stamp_rows // 2
    strip_rows = sky_ref.shape[0]

    @pl.when(step == 0)
    def _():
        copy = pltpu.make_async_copy(sky_ref, sky.at[pl.ds(0, strip_rows)], sem)
        copy.start()

        def build(m, carry):
            mats = []
            for k in range(terms):
                line = m * terms + k
                mat = band_matrix(rows_ref[pl.ds(line, 1), :], stamp_rows, half)
                mats.append(mat[:, :stamp_rows])
                col_ops[m, :, k * stamp_cols:(k + 1) * stamp_cols] = band_matrix(
                    cols_ref[pl.ds(line, 1), :], stamp_cols, half)
            row_ops[m] = jnp.concatenate(mats, axis=1)
            return carry

        lax.fori_loop(0, models, build, 0)
        sky[strip_rows:, :] = jnp.zeros((block_rows, sky.shape[1]), jnp.bfloat16)
        copy.wait()

    per_step = grads_ref.shape[0]

    def some(g, carry):
        done = []
        for u in range(group):
            local = g * group + u
            code = codes[step * per_step + local]
            model = code & ((1 << model_bits) - 1)
            block = code >> model_bits
            top = pl.multiple_of((block // col_blocks) * block_rows, block_rows)
            left = pl.multiple_of((block % col_blocks) * stamp_cols, stamp_cols)
            window = sky[pl.ds(top, stamp_rows), pl.ds(left, stamp_cols)]
            first = jnp.dot(window, col_ops[model],
                            preferred_element_type=jnp.float32).astype(jnp.bfloat16)
            tall = jnp.concatenate(
                [first[:, k * stamp_cols:(k + 1) * stamp_cols] for k in range(terms)], axis=0)
            out = jnp.dot(row_ops[model], tall, preferred_element_type=jnp.float32)
            done.append(out.astype(jnp.bfloat16))
        for u in range(group):
            grads_ref[g * group + u] = done[u]
        return carry

    lax.fori_loop(0, per_step // group, some, 0)


def divisor(number, wanted):
    return max(d for d in range(1, wanted + 1) if number % d == 0)


def in_place(stamps, tile_of, row_offset, col_offset, psf_model, psf_rows, psf_cols, cotangent):
    peers = lax.axis_size("tile")
    stamp_count, stamp_rows, stamp_cols = stamps.shape
    models, terms, taps = psf_rows.shape
    half = (taps - 1) // 2
    block_rows = stamp_rows // 2
    tile_rows, tile_cols = cotangent.shape
    row_blocks = tile_rows // block_rows
    col_blocks = tile_cols // stamp_cols
    strip_rows = peers * tile_rows
    model_bits = max(1, (models - 1).bit_length())
    upper = tile_of[:, 0] * row_blocks + row_offset
    codes = ((upper * col_blocks + col_offset) << model_bits) + psf_model
    lanes = 128
    per_step = divisor(stamp_count, 16)
    group = divisor(per_step, 8)
    grid = (stamp_count // per_step,)
    flops = 2 * stamp_count * terms * stamp_rows * stamp_cols * (stamp_rows + stamp_cols)
    smem = pl.BlockSpec(memory_space=pltpu.SMEM)
    table = pl.BlockSpec((models * terms, lanes), lambda i: (0, 0))
    pieces = pl.BlockSpec((per_step, stamp_rows, stamp_cols), lambda i: (i, 0, 0))
    params = pltpu.CompilerParams(vmem_limit_bytes=40 << 20)

    sky = lax.all_gather(cotangent, "tile", axis=0, tiled=True)
    strip = pl.pallas_call(
        partial(forward_kernel, half, terms, model_bits, col_blocks, group),
        grid=grid,
        out_shape=jax.ShapeDtypeStruct((strip_rows, tile_cols), jnp.bfloat16),
        in_specs=[smem, table, table, pieces],
        out_specs=pl.BlockSpec((strip_rows, tile_cols), lambda i: (0, 0)),
        scratch_shapes=[
            pltpu.VMEM((models, terms * stamp_rows, stamp_rows), jnp.bfloat16),
            pltpu.VMEM((models, terms * stamp_cols, stamp_cols), jnp.bfloat16),
            pltpu.VMEM((strip_rows + block_rows, tile_cols), jnp.float32),
        ],
        compiler_params=params,
        cost_estimate=pl.CostEstimate(flops=8 * flops, bytes_accessed=40 << 20, transcendentals=0),
    )(codes, tap_rows(psf_rows, lanes, False), tap_rows(psf_cols, lanes, True), stamps)
    tile_image = lax.psum_scatter(strip, "tile", scatter_dimension=0, tiled=True)
    stamp_grad = pl.pallas_call(
        partial(backward_kernel, half, terms, model_bits, col_blocks, group),
        grid=grid,
        out_shape=jax.ShapeDtypeStruct(stamps.shape, jnp.bfloat16),
        in_specs=[smem, table, table, pl.BlockSpec(memory_space=pl.ANY)],
        out_specs=pieces,
        scratch_shapes=[
            pltpu.VMEM((models, stamp_rows, terms * stamp_rows), jnp.bfloat16),
            pltpu.VMEM((models, stamp_cols, terms * stamp_cols), jnp.bfloat16),
            pltpu.VMEM((strip_rows + block_rows, tile_cols), jnp.bfloat16),
            pltpu.SemaphoreType.DMA,
        ],
        compiler_params=params,
        cost_estimate=pl.CostEstimate(flops=8 * flops, bytes_accessed=40 << 20, transcendentals=0),
    )(codes, tap_rows(psf_rows, lanes, True), tap_rows(psf_cols, lanes, False), sky)
    return tile_image, stamp_grad


def strip_fits(peers, cotangent):
    rows, cols = cotangent.shape
    return peers * rows * cols * 4 <= 12 << 20


def per_device_any(*args):
    if strip_fits(lax.axis_size("tile"), args[-1]):
        return in_place(*args)
    return per_device(*args)


def solution(mesh):
    in_specs = (
        P(("band", "tile"), None, None),
        P(("band", "tile"), None),
        P(("band", "tile")),
        P(("band", "tile")),
        P(("band", "tile")),
        P("band", None, None),
        P("band", None, None),
        P(("band", "tile"), None),
    )
    out_specs = (P(("band", "tile"), None), P(("band", "tile"), None, None))
    return jax.shard_map(
        per_device_any, mesh=mesh, in_specs=in_specs, out_specs=out_specs, check_vma=False
    )
```

```python
from functools import partial

import jax
import jax.numpy as jnp
from jax import lax
from jax.experimental import pallas as pl
from jax.experimental.pallas import tpu as pltpu
from jax.sharding import PartitionSpec as P


def passed_along(array, axis, by):
    peers = lax.axis_size(axis)
    pairs = [(i, i + by) for i in range(peers) if 0 <= i + by < peers]
    return lax.ppermute(array, axis, pairs)


def for_sending(array):

    def short(part):
        return part.astype(jnp.bfloat16) if part.dtype == jnp.float32 else part

    return jax.tree.map(short, array)


def band_table(taps_count, size):
    half_width = (taps_count - 1) // 2
    places = jnp.arange(size, dtype=jnp.int32)
    offsets = places[None, :] - places[:, None] + half_width
    taps_index = jnp.arange(taps_count, dtype=jnp.int32)
    table = (offsets[None, :, :] == taps_index[:, None, None]).astype(jnp.float32)
    return table.reshape((taps_count, size * size))


def build_ops(profiles, size):
    model_total, term_total, taps_count = profiles.shape
    table = band_table(taps_count, size)
    mats = jnp.dot(
        profiles.reshape((model_total * term_total, taps_count)),
        table,
        precision=lax.Precision.HIGHEST,
    )
    return mats.reshape((model_total, term_total, size, size)).astype(jnp.bfloat16)


def convolve_one(inputs, row_ops, col_ops):
    image, model = inputs
    row_mats = lax.dynamic_index_in_dim(row_ops, model, 0, keepdims=False)
    col_mats = lax.dynamic_index_in_dim(col_ops, model, 0, keepdims=False)
    row_pass = jnp.einsum(
        "kij,jx->kix", row_mats, image, preferred_element_type=jnp.float32
    ).astype(jnp.bfloat16)
    return jnp.einsum("kix,kyx->iy", row_pass, col_mats, preferred_element_type=jnp.float32).astype(
        jnp.bfloat16
    )


def transpose_one(inputs, row_ops, col_ops):
    window, model = inputs
    row_mats = lax.dynamic_index_in_dim(row_ops, model, 0, keepdims=False)
    col_mats = lax.dynamic_index_in_dim(col_ops, model, 0, keepdims=False)
    back_pass = jnp.einsum(
        "iy,kyx->kix", window, col_mats, preferred_element_type=jnp.float32
    ).astype(jnp.bfloat16)
    return jnp.einsum(
        "kji,kjx->ix", row_mats, back_pass, preferred_element_type=jnp.float32
    ).astype(jnp.bfloat16)


def apply_all(function, images, models, row_ops, col_ops):
    bound = partial(function, row_ops=row_ops, col_ops=col_ops)
    return lax.map(bound, (images, models.astype(jnp.int32)), batch_size=32)


def per_device(stamps, tile_of, row_offset, col_offset, psf_model, psf_rows, psf_cols, cotangent):
    peer_count = lax.axis_size("tile")
    stamp_count, stamp_rows, stamp_cols = stamps.shape
    block_rows = stamp_rows // 2
    tile_rows, tile_cols = cotangent.shape
    row_blocks = tile_rows // block_rows
    col_blocks = tile_cols // stamp_cols
    capacity = max(2, (5 * stamp_count + 4 * peer_count - 1) // (4 * peer_count))
    slot_total = peer_count * capacity
    row_ops = build_ops(psf_rows, stamp_rows)
    col_ops = build_ops(psf_cols, stamp_cols)
    target = tile_of[:, 0]
    order = jnp.arange(stamp_count, dtype=jnp.int32)
    earlier = (target[None, :] == target[:, None]) & (order[None, :] < order[:, None])
    slots = target * capacity + jnp.sum(earlier.astype(jnp.int32), axis=1)
    slot_ids = jnp.arange(slot_total, dtype=jnp.int32)
    matches = slots[None, :] == slot_ids[:, None]
    place = matches.astype(jnp.bfloat16)
    details = jnp.stack([jnp.ones_like(target), row_offset, col_offset, psf_model], axis=1)
    detail_send = jnp.sum(jnp.where(matches[:, :, None], details[None, :, :], 0), axis=1)
    detail_send = detail_send.reshape(peer_count, capacity, 4)
    raw_send = jnp.dot(
        place,
        stamps.reshape((stamp_count, stamp_rows * stamp_cols)),
        preferred_element_type=jnp.float32,
    )
    raw_send = raw_send.astype(jnp.bfloat16).reshape(peer_count, capacity, stamp_rows, stamp_cols)
    raw_part = lax.all_to_all(raw_send, "tile", split_axis=0, concat_axis=0, tiled=True)
    info_part = lax.all_to_all(detail_send, "tile", split_axis=0, concat_axis=0, tiled=True)
    flat = raw_part.reshape((-1, stamp_rows, stamp_cols))
    result = apply_all(convolve_one, flat, info_part.reshape((-1, 4))[:, 3], row_ops, col_ops)
    received = result.reshape(raw_part.shape)
    info_flat = info_part.reshape((slot_total, 4))
    upper_block = info_flat[:, 1]
    block_ids = jnp.stack([upper_block, upper_block + 1], axis=1) * col_blocks + info_flat[:, 2:3]
    targets = jnp.arange((row_blocks + 1) * col_blocks, dtype=jnp.int32)
    placing = (block_ids.reshape(-1)[None, :] == targets[:, None]).astype(jnp.bfloat16)
    pieces = received.reshape((slot_total * 2, block_rows * stamp_cols))
    extended = jnp.dot(placing, pieces, preferred_element_type=jnp.float32)
    extended = extended.reshape(row_blocks + 1, col_blocks, block_rows, stamp_cols).transpose(
        0, 2, 1, 3
    )
    extended = extended.reshape((row_blocks + 1) * block_rows, tile_cols)
    arriving = passed_along(extended[tile_rows:].astype(jnp.bfloat16), "tile", 1).astype(
        jnp.float32
    )
    tile_sum = extended[:tile_rows].at[:block_rows].add(arriving)
    tile_image = tile_sum.astype(jnp.bfloat16)
    rim = passed_along(cotangent[:block_rows], "tile", -1)
    padded = jnp.concatenate([cotangent, rim], axis=0)
    blocks = padded.reshape(row_blocks + 1, block_rows, col_blocks, stamp_cols).transpose(
        0, 2, 1, 3
    )
    blocks = blocks.reshape((row_blocks + 1) * col_blocks, block_rows * stamp_cols)
    windows = lax.dot_general(
        placing, blocks, (((0,), (0,)), ((), ())), preferred_element_type=jnp.float32
    )
    windows = windows.astype(jnp.bfloat16).reshape(slot_total, stamp_rows, stamp_cols)
    slot_grads = apply_all(transpose_one, windows, info_flat[:, 3], row_ops, col_ops)
    slot_grads = slot_grads.reshape(peer_count, capacity, stamp_rows, stamp_cols)
    returned = lax.all_to_all(
        for_sending(slot_grads), "tile", split_axis=0, concat_axis=0, tiled=True
    ).astype(slot_grads.dtype)
    stamp_grad = lax.dot_general(
        place,
        returned.reshape((slot_total, stamp_rows * stamp_cols)),
        (((0,), (0,)), ((), ())),
        preferred_element_type=jnp.float32,
    )
    stamp_grad = stamp_grad.astype(jnp.bfloat16).reshape(stamp_count, stamp_rows, stamp_cols)
    return (tile_image, stamp_grad)


MESH = pl.DeviceIdType.MESH


def band_matrix(taps, lanes):
    count = taps.shape[1]
    half = (count - 1) // 2
    row = jnp.concatenate([taps, jnp.zeros((1, lanes - count), jnp.float32)], axis=1)
    spread = jnp.broadcast_to(row, (lanes, lanes))
    turned = pltpu.roll(spread, lanes - half, 1, stride=1, stride_axis=0)
    down = lax.broadcasted_iota(jnp.int32, (lanes, lanes), 0)
    across = lax.broadcasted_iota(jnp.int32, (lanes, lanes), 1)
    return jnp.where(jnp.abs(across - down) <= half, turned, 0.0)


def build_kernel(rows_ref, cols_ref, cot_ref, row_fwd, row_bwd, col_fwd, col_bwd, blocks_ref):
    models, terms, _ = rows_ref.shape
    size = row_bwd.shape[1]
    lanes = col_bwd.shape[1]

    def build(m, carry):
        taps_rows, taps_cols = rows_ref[m], cols_ref[m]
        turned = []
        for k in range(terms):
            mat = band_matrix(taps_rows[k:k + 1], lanes)
            row_fwd[m, k * size:(k + 1) * size, :] = mat[:size, :size].astype(jnp.bfloat16)
            turned.append(mat.T[:size, :size].astype(jnp.bfloat16))
            mat = band_matrix(taps_cols[k:k + 1], lanes)
            col_bwd[m, :, k * lanes:(k + 1) * lanes] = mat.astype(jnp.bfloat16)
            col_fwd[m, k * lanes:(k + 1) * lanes, :] = mat.T.astype(jnp.bfloat16)
        row_bwd[m] = jnp.concatenate(turned, axis=1)
        return carry

    lax.fori_loop(0, models, build, 0)
    block_count, block_rows, stamp_cols = blocks_ref.shape
    across = cot_ref.shape[1] // stamp_cols
    for b in range(block_count):
        top, left = b // across * block_rows, b % across * stamp_cols
        blocks_ref[b] = cot_ref[top:top + block_rows, left:left + stamp_cols]


def add_kernel(model_bits, col_blocks, group, codes, conv_ref, strip_ref, total):
    count, stamp_rows, stamp_cols = conv_ref.shape
    block_rows = stamp_rows // 2
    strip_rows = strip_ref.shape[0]

    def clear(i, carry):
        spot = pl.ds(pl.multiple_of(i * block_rows, block_rows), block_rows)
        total[spot, :] = jnp.zeros((block_rows, total.shape[1]), jnp.float32)
        return carry

    lax.fori_loop(0, total.shape[0] // block_rows, clear, 0)

    def some(g, carry):
        for u in range(group):
            block = codes[g * group + u] >> model_bits
            top = pl.multiple_of((block // col_blocks) * block_rows, block_rows)
            left = pl.multiple_of((block % col_blocks) * stamp_cols, stamp_cols)
            spot = (pl.ds(top, stamp_rows), pl.ds(left, stamp_cols))
            total[spot] = total[spot] + conv_ref[g * group + u].astype(jnp.float32)
        return carry

    lax.fori_loop(0, count // group, some, 0)

    def put(i, carry):
        spot = pl.ds(pl.multiple_of(i * block_rows, block_rows), block_rows)
        strip_ref[spot, :] = total[spot, :].astype(jnp.bfloat16)
        return carry

    lax.fori_loop(0, strip_rows // block_rows, put, 0)


class Place:
    def __init__(self, peers):
        self.planes = peers // 4
        self.me = lax.axis_index("tile")
        self.core = lax.rem(self.me, 2)
        self.row = lax.rem(self.me // 2, 2)
        self.plane = self.me // 4

    def at(self, shift=0, row=0, core=0):
        plane = lax.rem(self.plane + shift + self.planes, self.planes)
        y = 1 - self.row if row else self.row
        c = 1 - self.core if core else self.core
        return plane * 4 + y * 2 + c

    def greet(self):
        barrier = pltpu.get_barrier_semaphore()
        others = [self.at(d) for d in range(1, self.planes)] + [self.at(row=1), self.at(core=1)]
        for other in others:
            pl.semaphore_signal(barrier, inc=1, device_id={"tile": other}, device_id_type=MESH)
        pl.semaphore_wait(barrier, len(others))


def remote(src, dst, send, recv, device):
    return pltpu.make_async_remote_copy(src_ref=src, dst_ref=dst, send_sem=send, recv_sem=recv,
                                        device_id={"tile": device}, device_id_type=MESH)


def forward_kernel(peers, terms, model_bits, group, codes, row_ops, col_ops, stamps_ref, cot_ref,
                   conv_ref, sky, own_sem, z_send, z_recv, y_send, y_recv, c_send, c_recv):
    place = Place(peers)
    planes = place.planes
    count, stamp_rows, stamp_cols = stamps_ref.shape
    groups = count // group

    def some(g, carry):
        for u in range(group):
            s = g * group + u
            model = codes[s] & ((1 << model_bits) - 1)
            first = jnp.dot(row_ops[model], stamps_ref[s],
                            preferred_element_type=jnp.float32).astype(jnp.bfloat16)
            wide = jnp.concatenate(
                [first[k * stamp_rows:(k + 1) * stamp_rows] for k in range(terms)], axis=1)
            conv_ref[s] = jnp.dot(wide, col_ops[model],
                                  preferred_element_type=jnp.float32).astype(jnp.bfloat16)
        return carry

    reached = [0]

    def compute(share):
        stop = min(groups, reached[0] + share)
        if stop > reached[0]:
            lax.fori_loop(reached[0], stop, some, 0)
        reached[0] = stop

    place.greet()
    own = pltpu.make_async_copy(cot_ref, sky.at[place.me], own_sem)
    own.start()
    to_z, to_y, to_c = {}, {}, {}
    for d in range(1, planes):
        to_z[d] = remote(cot_ref, sky.at[place.me], z_send.at[d], z_recv.at[d], place.at(d))
        to_z[d].start()
    to_y[0] = remote(cot_ref, sky.at[place.me], y_send.at[0], y_recv.at[0], place.at(row=1))
    to_y[0].start()
    to_c[0] = remote(cot_ref, sky.at[place.me], c_send.at[0], c_recv.at[0], place.at(core=1))
    to_c[0].start()
    compute(groups * 5 // 16)
    for d in range(1, planes):
        tile = sky.at[place.at(-d)]
        remote(tile, tile, z_send.at[d], z_recv.at[d], place.at(d)).wait_recv()
        to_y[d] = remote(tile, tile, y_send.at[d], y_recv.at[d], place.at(row=1))
        to_y[d].start()
        to_c[d] = remote(tile, tile, c_send.at[d], c_recv.at[d], place.at(core=1))
        to_c[d].start()
        compute(groups * 3 // 16)
    for d in range(planes):
        tile = sky.at[place.at(-d, row=1)]
        e = planes + d
        remote(tile, tile, y_send.at[d], y_recv.at[d], place.at(row=1)).wait_recv()
        to_c[e] = remote(tile, tile, c_send.at[e], c_recv.at[e], place.at(core=1))
        to_c[e].start()
        compute(groups // 16 if d < planes - 1 else groups)
    for e in range(2 * planes):
        tile = sky.at[place.at(-(e % planes), row=e // planes, core=1)]
        remote(tile, tile, c_send.at[e], c_recv.at[e], place.at(core=1)).wait_recv()
    own.wait()
    for copy in [*to_z.values(), *to_y.values(), *to_c.values()]:
        copy.wait_send()


def backward_kernel(peers, terms, model_bits, col_blocks, group, codes, row_ops, col_ops, sky_ref,
                    strip, grads_ref, tile_ref, sky, from_c, out_y, from_y, out_z, from_z,
                    own_sem, z_send, z_recv, y_send, y_recv, c_send, c_recv):
    place = Place(peers)
    planes = place.planes
    count, stamp_rows, stamp_cols = grads_ref.shape
    groups = count // group
    block_rows = stamp_rows // 2
    sky_blocks = sky_ref.shape[0]
    tile_rows = tile_ref.shape[0]

    def some(g, carry):
        for u in range(group):
            s = g * group + u
            code = codes[s]
            model = code & ((1 << model_bits) - 1)
            block = code >> model_bits
            window = jnp.concatenate([sky[block], sky[block + col_blocks]], axis=0)
            first = jnp.dot(window, col_ops[model],
                            preferred_element_type=jnp.float32).astype(jnp.bfloat16)
            tall = jnp.concatenate(
                [first[:, k * stamp_cols:(k + 1) * stamp_cols] for k in range(terms)], axis=0)
            grads_ref[s] = jnp.dot(row_ops[model], tall,
                                   preferred_element_type=jnp.float32).astype(jnp.bfloat16)
        return carry

    reached = [0]

    def compute(share):
        stop = min(groups, reached[0] + share)
        if stop > reached[0]:
            lax.fori_loop(reached[0], stop, some, 0)
        reached[0] = stop

    def summed(store, *parts):
        def body(i, carry):
            spot = pl.ds(pl.multiple_of(i * block_rows, block_rows), block_rows)
            out = parts[0][0][parts[0][1], spot, :].astype(jnp.float32)
            for ref, index in parts[1:]:
                out = out + ref[index, spot, :].astype(jnp.float32)
            store(spot, out.astype(jnp.bfloat16))
            return carry

        lax.fori_loop(0, tile_rows // block_rows, body, 0)

    own = pltpu.make_async_copy(sky_ref, sky.at[pl.ds(0, sky_blocks)], own_sem)
    own.start()
    place.greet()
    shifts = list(range(1, planes)) + [0]
    to_c, to_y, to_z = [], [], []
    for e in range(2 * planes):
        far = 1 if e < planes else 0
        source = strip.at[place.at(shifts[e % planes], row=far, core=1)]
        to_c.append(remote(source, from_c.at[e], c_send.at[e], c_recv.at[e], place.at(core=1)))
        to_c[-1].start()
    sky[sky_blocks:] = jnp.zeros((col_blocks, block_rows, stamp_cols), jnp.bfloat16)
    own.wait()
    for i in range(planes):
        to_c[i].wait_recv()

        def keep(spot, value, i=i):
            out_y[i, spot, :] = value

        summed(keep, (strip, place.at(shifts[i], row=1)), (from_c, i))
        to_y.append(remote(out_y.at[i], from_y.at[i], y_send.at[i], y_recv.at[i], place.at(row=1)))
        to_y[-1].start()
        compute(groups // 16)
    for i in range(planes):
        to_c[planes + i].wait_recv()
        to_y[i].wait_recv()
        if i == planes - 1:
            break

        def keep(spot, value, i=i):
            out_z[i, spot, :] = value

        summed(keep, (strip, place.at(shifts[i])), (from_c, planes + i), (from_y, i))
        to_z.append(remote(out_z.at[i], from_z.at[i], z_send.at[i], z_recv.at[i],
                           place.at(shifts[i])))
        to_z[-1].start()
        compute(groups * 3 // 16)
    compute(groups)
    for copy in to_z:
        copy.wait_recv()

    def keep(spot, value):
        tile_ref[spot, :] = value

    summed(keep, (strip, place.me), (from_c, 2 * planes - 1), (from_y, planes - 1),
           *[(from_z, i) for i in range(planes - 1)])
    for copy in to_c + to_y + to_z:
        copy.wait_send()


def divisor(number, wanted):
    return max(d for d in range(1, wanted + 1) if number % d == 0)


def in_place(stamps, tile_of, row_offset, col_offset, psf_model, psf_rows, psf_cols, cotangent):
    peers = lax.axis_size("tile")
    planes = peers // 4
    stamp_count, stamp_rows, stamp_cols = stamps.shape
    models, terms, taps = psf_rows.shape
    block_rows = stamp_rows // 2
    tile_rows, tile_cols = cotangent.shape
    row_blocks = tile_rows // block_rows
    col_blocks = tile_cols // stamp_cols
    strip_rows = peers * tile_rows
    model_bits = max(1, (models - 1).bit_length())
    upper = tile_of[:, 0] * row_blocks + row_offset
    codes = ((upper * col_blocks + col_offset) << model_bits) + psf_model
    group = divisor(stamp_count, 8)
    flops = 2 * stamp_count * terms * stamp_rows * stamp_cols * (stamp_rows + stamp_cols)
    cost = pl.CostEstimate(flops=8 * flops, bytes_accessed=40 << 20, transcendentals=0)
    smem = pl.BlockSpec(memory_space=pltpu.SMEM)
    vmem = pl.BlockSpec(memory_space=pltpu.VMEM)
    anywhere = pl.BlockSpec(memory_space=pl.ANY)
    short = jnp.bfloat16
    dma = pltpu.SemaphoreType.DMA
    limit = 44 << 20
    block_shape = (row_blocks * col_blocks, block_rows, stamp_cols)

    row_fwd, row_bwd, col_fwd, col_bwd, blocks = pl.pallas_call(
        build_kernel,
        out_shape=(
            jax.ShapeDtypeStruct((models, terms * stamp_rows, stamp_rows), short),
            jax.ShapeDtypeStruct((models, stamp_rows, terms * stamp_rows), short),
            jax.ShapeDtypeStruct((models, terms * stamp_cols, stamp_cols), short),
            jax.ShapeDtypeStruct((models, stamp_cols, terms * stamp_cols), short),
            jax.ShapeDtypeStruct(block_shape, short),
        ),
        in_specs=[vmem] * 3,
        out_specs=(vmem,) * 5,
        compiler_params=pltpu.CompilerParams(vmem_limit_bytes=limit),
    )(psf_rows, psf_cols, cotangent)
    conv, sky = pl.pallas_call(
        partial(forward_kernel, peers, terms, model_bits, group),
        out_shape=(
            jax.ShapeDtypeStruct(stamps.shape, short),
            jax.ShapeDtypeStruct((peers,) + block_shape, short),
        ),
        in_specs=[smem, vmem, vmem, vmem, anywhere],
        out_specs=(vmem, anywhere),
        scratch_shapes=[dma, dma((planes,)), dma((planes,)), dma((planes,)), dma((planes,)),
                        dma((2 * planes,)), dma((2 * planes,))],
        compiler_params=pltpu.CompilerParams(collective_id=0, has_side_effects=True,
                                             vmem_limit_bytes=limit),
        cost_estimate=cost,
    )(codes, row_fwd, col_fwd, stamps, blocks)
    strip = pl.pallas_call(
        partial(add_kernel, model_bits, col_blocks, group),
        out_shape=jax.ShapeDtypeStruct((strip_rows, tile_cols), short),
        in_specs=[smem, vmem],
        out_specs=vmem,
        scratch_shapes=[pltpu.VMEM((strip_rows + block_rows, tile_cols), jnp.float32)],
        compiler_params=pltpu.CompilerParams(vmem_limit_bytes=limit),
    )(codes, conv)
    tile = (tile_rows, tile_cols)
    stamp_grad, tile_image = pl.pallas_call(
        partial(backward_kernel, peers, terms, model_bits, col_blocks, group),
        out_shape=(
            jax.ShapeDtypeStruct(stamps.shape, short),
            jax.ShapeDtypeStruct(tile, short),
        ),
        in_specs=[smem, vmem, vmem, anywhere, vmem],
        out_specs=(vmem, vmem),
        scratch_shapes=[
            pltpu.VMEM(((peers * row_blocks + 1) * col_blocks,) + block_shape[1:], short),
            pltpu.VMEM((2 * planes,) + tile, short),
            pltpu.VMEM((planes,) + tile, short),
            pltpu.VMEM((planes,) + tile, short),
            pltpu.VMEM((planes,) + tile, short),
            pltpu.VMEM((planes,) + tile, short),
            dma, dma((planes,)), dma((planes,)), dma((planes,)), dma((planes,)),
            dma((2 * planes,)), dma((2 * planes,)),
        ],
        compiler_params=pltpu.CompilerParams(collective_id=1, has_side_effects=True,
                                             vmem_limit_bytes=limit),
        cost_estimate=cost,
    )(codes, row_bwd, col_bwd, sky.reshape((-1,) + block_shape[1:]),
      strip.reshape((peers,) + tile))
    return tile_image, stamp_grad


def strip_fits(peers, cotangent):
    rows, cols = cotangent.shape
    return peers % 4 == 0 and peers >= 8 and peers * rows * cols * 4 <= 12 << 20


def per_device_any(*args):
    if strip_fits(lax.axis_size("tile"), args[-1]):
        return in_place(*args)
    return per_device(*args)


def solution(mesh):
    in_specs = (
        P(("band", "tile"), None, None),
        P(("band", "tile"), None),
        P(("band", "tile")),
        P(("band", "tile")),
        P(("band", "tile")),
        P("band", None, None),
        P("band", None, None),
        P(("band", "tile"), None),
    )
    out_specs = (P(("band", "tile"), None), P(("band", "tile"), None, None))
    return jax.shard_map(
        per_device_any, mesh=mesh, in_specs=in_specs, out_specs=out_specs, check_vma=False
    )
```

```python
from functools import partial

import jax
import jax.numpy as jnp
from jax import lax
from jax.experimental import pallas as pl
from jax.experimental.pallas import tpu as pltpu
from jax.sharding import PartitionSpec as P


def passed_along(array, axis, by):
    peers = lax.axis_size(axis)
    pairs = [(i, i + by) for i in range(peers) if 0 <= i + by < peers]
    return lax.ppermute(array, axis, pairs)


def for_sending(array):

    def short(part):
        return part.astype(jnp.bfloat16) if part.dtype == jnp.float32 else part

    return jax.tree.map(short, array)


def band_table(taps_count, size):
    half_width = (taps_count - 1) // 2
    places = jnp.arange(size, dtype=jnp.int32)
    offsets = places[None, :] - places[:, None] + half_width
    taps_index = jnp.arange(taps_count, dtype=jnp.int32)
    table = (offsets[None, :, :] == taps_index[:, None, None]).astype(jnp.float32)
    return table.reshape((taps_count, size * size))


def build_ops(profiles, size):
    model_total, term_total, taps_count = profiles.shape
    table = band_table(taps_count, size)
    mats = jnp.dot(
        profiles.reshape((model_total * term_total, taps_count)),
        table,
        precision=lax.Precision.HIGHEST,
    )
    return mats.reshape((model_total, term_total, size, size)).astype(jnp.bfloat16)


def convolve_one(inputs, row_ops, col_ops):
    image, model = inputs
    row_mats = lax.dynamic_index_in_dim(row_ops, model, 0, keepdims=False)
    col_mats = lax.dynamic_index_in_dim(col_ops, model, 0, keepdims=False)
    row_pass = jnp.einsum(
        "kij,jx->kix", row_mats, image, preferred_element_type=jnp.float32
    ).astype(jnp.bfloat16)
    return jnp.einsum("kix,kyx->iy", row_pass, col_mats, preferred_element_type=jnp.float32).astype(
        jnp.bfloat16
    )


def transpose_one(inputs, row_ops, col_ops):
    window, model = inputs
    row_mats = lax.dynamic_index_in_dim(row_ops, model, 0, keepdims=False)
    col_mats = lax.dynamic_index_in_dim(col_ops, model, 0, keepdims=False)
    back_pass = jnp.einsum(
        "iy,kyx->kix", window, col_mats, preferred_element_type=jnp.float32
    ).astype(jnp.bfloat16)
    return jnp.einsum(
        "kji,kjx->ix", row_mats, back_pass, preferred_element_type=jnp.float32
    ).astype(jnp.bfloat16)


def apply_all(function, images, models, row_ops, col_ops):
    bound = partial(function, row_ops=row_ops, col_ops=col_ops)
    return lax.map(bound, (images, models.astype(jnp.int32)), batch_size=32)


def per_device(stamps, tile_of, row_offset, col_offset, psf_model, psf_rows, psf_cols, cotangent):
    peer_count = lax.axis_size("tile")
    stamp_count, stamp_rows, stamp_cols = stamps.shape
    block_rows = stamp_rows // 2
    tile_rows, tile_cols = cotangent.shape
    row_blocks = tile_rows // block_rows
    col_blocks = tile_cols // stamp_cols
    capacity = max(2, (5 * stamp_count + 4 * peer_count - 1) // (4 * peer_count))
    slot_total = peer_count * capacity
    row_ops = build_ops(psf_rows, stamp_rows)
    col_ops = build_ops(psf_cols, stamp_cols)
    target = tile_of[:, 0]
    order = jnp.arange(stamp_count, dtype=jnp.int32)
    earlier = (target[None, :] == target[:, None]) & (order[None, :] < order[:, None])
    slots = target * capacity + jnp.sum(earlier.astype(jnp.int32), axis=1)
    slot_ids = jnp.arange(slot_total, dtype=jnp.int32)
    matches = slots[None, :] == slot_ids[:, None]
    place = matches.astype(jnp.bfloat16)
    details = jnp.stack([jnp.ones_like(target), row_offset, col_offset, psf_model], axis=1)
    detail_send = jnp.sum(jnp.where(matches[:, :, None], details[None, :, :], 0), axis=1)
    detail_send = detail_send.reshape(peer_count, capacity, 4)
    raw_send = jnp.dot(
        place,
        stamps.reshape((stamp_count, stamp_rows * stamp_cols)),
        preferred_element_type=jnp.float32,
    )
    raw_send = raw_send.astype(jnp.bfloat16).reshape(peer_count, capacity, stamp_rows, stamp_cols)
    raw_part = lax.all_to_all(raw_send, "tile", split_axis=0, concat_axis=0, tiled=True)
    info_part = lax.all_to_all(detail_send, "tile", split_axis=0, concat_axis=0, tiled=True)
    flat = raw_part.reshape((-1, stamp_rows, stamp_cols))
    result = apply_all(convolve_one, flat, info_part.reshape((-1, 4))[:, 3], row_ops, col_ops)
    received = result.reshape(raw_part.shape)
    info_flat = info_part.reshape((slot_total, 4))
    upper_block = info_flat[:, 1]
    block_ids = jnp.stack([upper_block, upper_block + 1], axis=1) * col_blocks + info_flat[:, 2:3]
    targets = jnp.arange((row_blocks + 1) * col_blocks, dtype=jnp.int32)
    placing = (block_ids.reshape(-1)[None, :] == targets[:, None]).astype(jnp.bfloat16)
    pieces = received.reshape((slot_total * 2, block_rows * stamp_cols))
    extended = jnp.dot(placing, pieces, preferred_element_type=jnp.float32)
    extended = extended.reshape(row_blocks + 1, col_blocks, block_rows, stamp_cols).transpose(
        0, 2, 1, 3
    )
    extended = extended.reshape((row_blocks + 1) * block_rows, tile_cols)
    arriving = passed_along(extended[tile_rows:].astype(jnp.bfloat16), "tile", 1).astype(
        jnp.float32
    )
    tile_sum = extended[:tile_rows].at[:block_rows].add(arriving)
    tile_image = tile_sum.astype(jnp.bfloat16)
    rim = passed_along(cotangent[:block_rows], "tile", -1)
    padded = jnp.concatenate([cotangent, rim], axis=0)
    blocks = padded.reshape(row_blocks + 1, block_rows, col_blocks, stamp_cols).transpose(
        0, 2, 1, 3
    )
    blocks = blocks.reshape((row_blocks + 1) * col_blocks, block_rows * stamp_cols)
    windows = lax.dot_general(
        placing, blocks, (((0,), (0,)), ((), ())), preferred_element_type=jnp.float32
    )
    windows = windows.astype(jnp.bfloat16).reshape(slot_total, stamp_rows, stamp_cols)
    slot_grads = apply_all(transpose_one, windows, info_flat[:, 3], row_ops, col_ops)
    slot_grads = slot_grads.reshape(peer_count, capacity, stamp_rows, stamp_cols)
    returned = lax.all_to_all(
        for_sending(slot_grads), "tile", split_axis=0, concat_axis=0, tiled=True
    ).astype(slot_grads.dtype)
    stamp_grad = lax.dot_general(
        place,
        returned.reshape((slot_total, stamp_rows * stamp_cols)),
        (((0,), (0,)), ((), ())),
        preferred_element_type=jnp.float32,
    )
    stamp_grad = stamp_grad.astype(jnp.bfloat16).reshape(stamp_count, stamp_rows, stamp_cols)
    return (tile_image, stamp_grad)


MESH = pl.DeviceIdType.MESH


def band_matrix(taps, lanes):
    count = taps.shape[1]
    half = (count - 1) // 2
    row = jnp.concatenate([taps, jnp.zeros((1, lanes - count), jnp.float32)], axis=1)
    spread = jnp.broadcast_to(row, (lanes, lanes))
    turned = pltpu.roll(spread, lanes - half, 1, stride=1, stride_axis=0)
    down = lax.broadcasted_iota(jnp.int32, (lanes, lanes), 0)
    across = lax.broadcasted_iota(jnp.int32, (lanes, lanes), 1)
    return jnp.where(jnp.abs(across - down) <= half, turned, 0.0)


def build_kernel(rows_ref, cols_ref, cot_ref, row_fwd, row_bwd, col_fwd, col_bwd, blocks_ref):
    models, terms, _ = rows_ref.shape
    size = row_bwd.shape[1]
    lanes = col_bwd.shape[1]

    def build(m, carry):
        taps_rows, taps_cols = rows_ref[m], cols_ref[m]
        turned = []
        for k in range(terms):
            mat = band_matrix(taps_rows[k:k + 1], lanes)
            row_fwd[m, k * size:(k + 1) * size, :] = mat[:size, :size].astype(jnp.bfloat16)
            turned.append(mat.T[:size, :size].astype(jnp.bfloat16))
            mat = band_matrix(taps_cols[k:k + 1], lanes)
            col_bwd[m, :, k * lanes:(k + 1) * lanes] = mat.astype(jnp.bfloat16)
            col_fwd[m, k * lanes:(k + 1) * lanes, :] = mat.T.astype(jnp.bfloat16)
        row_bwd[m] = jnp.concatenate(turned, axis=1)
        return carry

    lax.fori_loop(0, models, build, 0)
    block_count, block_rows, stamp_cols = blocks_ref.shape
    across = cot_ref.shape[1] // stamp_cols
    for b in range(block_count):
        top, left = b // across * block_rows, b % across * stamp_cols
        blocks_ref[b] = cot_ref[top:top + block_rows, left:left + stamp_cols]


def add_kernel(model_bits, col_blocks, group, codes, conv_ref, strip_ref, total):
    count, stamp_rows, stamp_cols = conv_ref.shape
    block_rows = stamp_rows // 2
    strip_rows = strip_ref.shape[0]

    def clear(i, carry):
        spot = pl.ds(pl.multiple_of(i * block_rows, block_rows), block_rows)
        total[spot, :] = jnp.zeros((block_rows, total.shape[1]), jnp.float32)
        return carry

    lax.fori_loop(0, total.shape[0] // block_rows, clear, 0)

    def some(g, carry):
        for u in range(group):
            block = codes[g * group + u] >> model_bits
            top = pl.multiple_of((block // col_blocks) * block_rows, block_rows)
            left = pl.multiple_of((block % col_blocks) * stamp_cols, stamp_cols)
            spot = (pl.ds(top, stamp_rows), pl.ds(left, stamp_cols))
            total[spot] = total[spot] + conv_ref[g * group + u].astype(jnp.float32)
        return carry

    lax.fori_loop(0, count // group, some, 0)

    def put(i, carry):
        spot = pl.ds(pl.multiple_of(i * block_rows, block_rows), block_rows)
        strip_ref[spot, :] = total[spot, :].astype(jnp.bfloat16)
        return carry

    lax.fori_loop(0, strip_rows // block_rows, put, 0)


class Place:
    def __init__(self, peers):
        self.planes = peers // 4
        self.me = lax.axis_index("tile")
        self.core = lax.rem(self.me, 2)
        self.row = lax.rem(self.me // 2, 2)
        self.plane = self.me // 4

    def at(self, shift=0, row=0, core=0):
        plane = lax.rem(self.plane + shift + self.planes, self.planes)
        y = 1 - self.row if row else self.row
        c = 1 - self.core if core else self.core
        return plane * 4 + y * 2 + c

    def greet(self):
        barrier = pltpu.get_barrier_semaphore()
        others = [self.at(d) for d in range(1, self.planes)] + [self.at(row=1), self.at(core=1)]
        for other in others:
            pl.semaphore_signal(barrier, inc=1, device_id={"tile": other}, device_id_type=MESH)
        pl.semaphore_wait(barrier, len(others))


def remote(src, dst, send, recv, device):
    return pltpu.make_async_remote_copy(src_ref=src, dst_ref=dst, send_sem=send, recv_sem=recv,
                                        device_id={"tile": device}, device_id_type=MESH)


def forward_kernel(peers, terms, model_bits, group, codes, row_ops, col_ops, stamps_ref, cot_ref,
                   conv_ref, sky, own_sem, z_send, z_recv, y_send, y_recv, c_send, c_recv):
    place = Place(peers)
    planes = place.planes
    count, stamp_rows, stamp_cols = stamps_ref.shape
    groups = count // group

    def some(g, carry):
        for u in range(group):
            s = g * group + u
            model = codes[s] & ((1 << model_bits) - 1)
            first = jnp.dot(row_ops[model], stamps_ref[s],
                            preferred_element_type=jnp.float32).astype(jnp.bfloat16)
            wide = jnp.concatenate(
                [first[k * stamp_rows:(k + 1) * stamp_rows] for k in range(terms)], axis=1)
            conv_ref[s] = jnp.dot(wide, col_ops[model],
                                  preferred_element_type=jnp.float32).astype(jnp.bfloat16)
        return carry

    reached = [0]

    def compute(share):
        stop = min(groups, reached[0] + share)
        if stop > reached[0]:
            lax.fori_loop(reached[0], stop, some, 0)
        reached[0] = stop

    sky[peers] = jnp.zeros(sky.shape[1:], jnp.bfloat16)
    place.greet()
    own = pltpu.make_async_copy(cot_ref, sky.at[place.me], own_sem)
    own.start()
    p = place.plane
    last = planes - 1

    def z_copy(tile, source, slot, step):
        return remote(source, sky.at[tile], z_send.at[slot], z_recv.at[slot], place.at(step))

    def y_copy(tile, source, slot):
        return remote(source, sky.at[tile], y_send.at[slot], y_recv.at[slot], place.at(row=1))

    def c_copy(tile, source, slot):
        return remote(source, sky.at[tile], c_send.at[slot], c_recv.at[slot], place.at(core=1))

    def streams(i, body):
        pl.when(p >= i)(lambda: body(-i, i, 1, p < last))
        pl.when(p + i <= last)(lambda: body(i, last + i, -1, p > 0))

    pl.when(p < last)(lambda: z_copy(place.me, cot_ref, 1, 1).start())
    pl.when(p > 0)(lambda: z_copy(place.me, cot_ref, last + 1, -1).start())
    y_copy(place.me, cot_ref, 0).start()
    c_copy(place.me, cot_ref, 0).start()
    compute(groups * 4 // 16)
    for i in range(1, planes):

        def arrived(shift, slot, step, more):
            tile = place.at(shift)
            source = sky.at[tile]
            z_copy(tile, source, slot, step).wait_recv()
            if i < last:
                pl.when(more)(lambda: z_copy(tile, source, slot + 1, step).start())
            y_copy(tile, source, slot).start()
            c_copy(tile, source, slot).start()

        streams(i, arrived)
        compute(groups * 3 // 16 if i < last else groups)

    half = 2 * last + 1

    def crossed(shift, slot):
        tile = place.at(shift, row=1)
        y_copy(tile, sky.at[tile], slot).wait_recv()
        c_copy(tile, sky.at[tile], half + slot).start()

    def finished(shift, slot):
        for row in range(2):
            tile = place.at(shift, row=row, core=1)
            c_copy(tile, sky.at[tile], row * half + slot).wait_recv()
            c_copy(tile, sky.at[tile], row * half + slot).wait_send()
        y_copy(tile, sky.at[tile], slot).wait_send()

    crossed(0, 0)
    for i in range(1, planes):
        streams(i, lambda shift, slot, step, more: crossed(shift, slot))
    finished(0, 0)
    own.wait()
    pl.when(p < last)(lambda: z_copy(place.me, cot_ref, 1, 1).wait_send())
    pl.when(p > 0)(lambda: z_copy(place.me, cot_ref, last + 1, -1).wait_send())
    for i in range(1, planes):

        def ended(shift, slot, step, more):
            finished(shift, slot)
            if i < last:
                tile = place.at(shift)
                pl.when(more)(lambda: z_copy(tile, sky.at[tile], slot + 1, step).wait_send())

        streams(i, ended)


def backward_kernel(peers, terms, model_bits, col_blocks, group, codes, row_ops, col_ops, sky,
                    strip, grads_ref, tile_ref, from_c, out_y, from_y, out_z, from_z,
                    z_send, z_recv, y_send, y_recv, c_send, c_recv):
    place = Place(peers)
    planes = place.planes
    count, stamp_rows, stamp_cols = grads_ref.shape
    groups = count // group
    block_rows = stamp_rows // 2
    tile_rows = tile_ref.shape[0]

    def some(g, carry):
        for u in range(group):
            s = g * group + u
            code = codes[s]
            model = code & ((1 << model_bits) - 1)
            block = code >> model_bits
            window = jnp.concatenate([sky[block], sky[block + col_blocks]], axis=0)
            first = jnp.dot(window, col_ops[model],
                            preferred_element_type=jnp.float32).astype(jnp.bfloat16)
            tall = jnp.concatenate(
                [first[:, k * stamp_cols:(k + 1) * stamp_cols] for k in range(terms)], axis=0)
            grads_ref[s] = jnp.dot(row_ops[model], tall,
                                   preferred_element_type=jnp.float32).astype(jnp.bfloat16)
        return carry

    reached = [0]

    def compute(share):
        stop = min(groups, reached[0] + share)
        if stop > reached[0]:
            lax.fori_loop(reached[0], stop, some, 0)
        reached[0] = stop

    def summed(store, *parts):
        def body(i, carry):
            spot = pl.ds(pl.multiple_of(i * block_rows, block_rows), block_rows)
            out = parts[0][0][parts[0][1], spot, :].astype(jnp.float32)
            for ref, index in parts[1:]:
                out = out + ref[index, spot, :].astype(jnp.float32)
            store(spot, out.astype(jnp.bfloat16))
            return carry

        lax.fori_loop(0, tile_rows // block_rows, body, 0)

    place.greet()
    p = place.plane
    last = planes - 1
    upper = p // 2
    mirrored = (1 - 2 * upper) * p + last * upper
    targets = [last * upper + (1 - 2 * upper) * q for q in (3, 2, 1 - mirrored, mirrored)]
    shifts = [q - p for q in targets]
    to_c, to_y = [], []
    for e in range(2 * planes):
        far = 1 if e < planes else 0
        source = strip.at[place.at(shifts[e % planes], row=far, core=1)]
        to_c.append(remote(source, from_c.at[e], c_send.at[e], c_recv.at[e], place.at(core=1)))
        to_c[-1].start()
    for i in range(planes):
        to_c[i].wait_recv()

        def keep(spot, value, i=i):
            out_y[i, spot, :] = value

        summed(keep, (strip, place.at(shifts[i], row=1)), (from_c, i))
        to_y.append(remote(out_y.at[i], from_y.at[i], y_send.at[i], y_recv.at[i], place.at(row=1)))
        to_y[-1].start()
    compute(groups * 4 // 16)

    def z_copy(i, slot, step):
        return remote(out_z.at[i], from_z.at[slot], z_send.at[i], z_recv.at[slot], place.at(step))

    for i in range(last):
        to_c[planes + i].wait_recv()
        to_y[i].wait_recv()
        target = targets[i]
        parts = [(strip, place.at(shifts[i])), (from_c, planes + i), (from_y, i)]

        def keep(spot, value):
            out_z[i, spot, :] = value

        def pass_on(slot, step, first):
            @pl.when(first)
            def _():
                summed(keep, *parts)

            @pl.when(jnp.logical_not(first))
            def _():
                z_copy(i, slot, step).wait_recv()
                summed(keep, *parts, (from_z, slot))

            z_copy(i, slot, step).start()

        pl.when(target > p)(lambda: pass_on(target, 1, p == 0))
        pl.when(target < p)(lambda: pass_on(planes + target, -1, p == last))
        compute(groups * 3 // 16)
    compute(groups)
    to_c[2 * planes - 1].wait_recv()
    to_y[last].wait_recv()
    parts = [(strip, place.me), (from_c, 2 * planes - 1), (from_y, last)]

    def finish(*slots):
        for slot in slots:
            z_copy(0, slot, 1).wait_recv()

        def keep(spot, value):
            tile_ref[spot, :] = value

        summed(keep, *parts, *[(from_z, slot) for slot in slots])

    pl.when(p == 0)(lambda: finish(planes + p))
    pl.when(p == last)(lambda: finish(p))
    pl.when(jnp.logical_and(p > 0, p < last))(lambda: finish(p, planes + p))
    for copy in to_c + to_y:
        copy.wait_send()
    for i in range(last):
        z_copy(i, i, 1).wait_send()


def divisor(number, wanted):
    return max(d for d in range(1, wanted + 1) if number % d == 0)


def in_place(stamps, tile_of, row_offset, col_offset, psf_model, psf_rows, psf_cols, cotangent):
    peers = lax.axis_size("tile")
    planes = peers // 4
    stamp_count, stamp_rows, stamp_cols = stamps.shape
    models, terms, taps = psf_rows.shape
    block_rows = stamp_rows // 2
    tile_rows, tile_cols = cotangent.shape
    row_blocks = tile_rows // block_rows
    col_blocks = tile_cols // stamp_cols
    strip_rows = peers * tile_rows
    model_bits = max(1, (models - 1).bit_length())
    upper = tile_of[:, 0] * row_blocks + row_offset
    codes = ((upper * col_blocks + col_offset) << model_bits) + psf_model
    group = divisor(stamp_count, 8)
    flops = 2 * stamp_count * terms * stamp_rows * stamp_cols * (stamp_rows + stamp_cols)
    cost = pl.CostEstimate(flops=8 * flops, bytes_accessed=40 << 20, transcendentals=0)
    smem = pl.BlockSpec(memory_space=pltpu.SMEM)
    vmem = pl.BlockSpec(memory_space=pltpu.VMEM)
    anywhere = pl.BlockSpec(memory_space=pl.ANY)
    short = jnp.bfloat16
    dma = pltpu.SemaphoreType.DMA
    limit = 44 << 20
    block_shape = (row_blocks * col_blocks, block_rows, stamp_cols)

    row_fwd, row_bwd, col_fwd, col_bwd, blocks = pl.pallas_call(
        build_kernel,
        out_shape=(
            jax.ShapeDtypeStruct((models, terms * stamp_rows, stamp_rows), short),
            jax.ShapeDtypeStruct((models, stamp_rows, terms * stamp_rows), short),
            jax.ShapeDtypeStruct((models, terms * stamp_cols, stamp_cols), short),
            jax.ShapeDtypeStruct((models, stamp_cols, terms * stamp_cols), short),
            jax.ShapeDtypeStruct(block_shape, short),
        ),
        in_specs=[vmem] * 3,
        out_specs=(vmem,) * 5,
        compiler_params=pltpu.CompilerParams(vmem_limit_bytes=limit),
    )(psf_rows, psf_cols, cotangent)
    conv, sky = pl.pallas_call(
        partial(forward_kernel, peers, terms, model_bits, group),
        out_shape=(
            jax.ShapeDtypeStruct(stamps.shape, short),
            jax.ShapeDtypeStruct((peers + 1,) + block_shape, short),
        ),
        in_specs=[smem, vmem, vmem, vmem, anywhere],
        out_specs=(vmem, vmem),
        scratch_shapes=[dma] + [dma((2 * planes - 1,))] * 4 + [dma((4 * planes - 2,))] * 2,
        compiler_params=pltpu.CompilerParams(collective_id=0, has_side_effects=True,
                                             vmem_limit_bytes=limit),
        cost_estimate=cost,
    )(codes, row_fwd, col_fwd, stamps, blocks)
    strip = pl.pallas_call(
        partial(add_kernel, model_bits, col_blocks, group),
        out_shape=jax.ShapeDtypeStruct((strip_rows, tile_cols), short),
        in_specs=[smem, vmem],
        out_specs=vmem,
        scratch_shapes=[pltpu.VMEM((strip_rows + block_rows, tile_cols), jnp.float32)],
        compiler_params=pltpu.CompilerParams(vmem_limit_bytes=limit),
    )(codes, conv)
    tile = (tile_rows, tile_cols)
    stamp_grad, tile_image = pl.pallas_call(
        partial(backward_kernel, peers, terms, model_bits, col_blocks, group),
        out_shape=(
            jax.ShapeDtypeStruct(stamps.shape, short),
            jax.ShapeDtypeStruct(tile, short),
        ),
        in_specs=[smem, vmem, vmem, vmem, vmem],
        out_specs=(vmem, vmem),
        scratch_shapes=[
            pltpu.VMEM((2 * planes,) + tile, short),
            pltpu.VMEM((planes,) + tile, short),
            pltpu.VMEM((planes,) + tile, short),
            pltpu.VMEM((planes,) + tile, short),
            pltpu.VMEM((2 * planes,) + tile, short),
            dma((planes,)), dma((2 * planes,)), dma((planes,)), dma((planes,)),
            dma((2 * planes,)), dma((2 * planes,)),
        ],
        compiler_params=pltpu.CompilerParams(collective_id=1, has_side_effects=True,
                                             vmem_limit_bytes=limit),
        cost_estimate=cost,
    )(codes, row_bwd, col_bwd, sky.reshape((-1,) + block_shape[1:]),
      strip.reshape((peers,) + tile))
    return tile_image, stamp_grad


def strip_fits(peers, cotangent):
    rows, cols = cotangent.shape
    return peers == 16 and peers * rows * cols * 4 <= 12 << 20


def per_device_any(*args):
    if strip_fits(lax.axis_size("tile"), args[-1]):
        return in_place(*args)
    return per_device(*args)


def solution(mesh):
    in_specs = (
        P(("band", "tile"), None, None),
        P(("band", "tile"), None),
        P(("band", "tile")),
        P(("band", "tile")),
        P(("band", "tile")),
        P("band", None, None),
        P("band", None, None),
        P(("band", "tile"), None),
    )
    out_specs = (P(("band", "tile"), None), P(("band", "tile"), None, None))
    return jax.shard_map(
        per_device_any, mesh=mesh, in_specs=in_specs, out_specs=out_specs, check_vma=False
    )
```

```python
from functools import partial

import jax
import jax.numpy as jnp
from jax import lax
from jax.experimental import pallas as pl
from jax.experimental.pallas import tpu as pltpu
from jax.sharding import PartitionSpec as P


def passed_along(array, axis, by):
    peers = lax.axis_size(axis)
    pairs = [(i, i + by) for i in range(peers) if 0 <= i + by < peers]
    return lax.ppermute(array, axis, pairs)


def for_sending(array):

    def short(part):
        return part.astype(jnp.bfloat16) if part.dtype == jnp.float32 else part

    return jax.tree.map(short, array)


def band_table(taps_count, size):
    half_width = (taps_count - 1) // 2
    places = jnp.arange(size, dtype=jnp.int32)
    offsets = places[None, :] - places[:, None] + half_width
    taps_index = jnp.arange(taps_count, dtype=jnp.int32)
    table = (offsets[None, :, :] == taps_index[:, None, None]).astype(jnp.float32)
    return table.reshape((taps_count, size * size))


def build_ops(profiles, size):
    model_total, term_total, taps_count = profiles.shape
    table = band_table(taps_count, size)
    mats = jnp.dot(
        profiles.reshape((model_total * term_total, taps_count)),
        table,
        precision=lax.Precision.HIGHEST,
    )
    return mats.reshape((model_total, term_total, size, size)).astype(jnp.bfloat16)


def convolve_one(inputs, row_ops, col_ops):
    image, model = inputs
    row_mats = lax.dynamic_index_in_dim(row_ops, model, 0, keepdims=False)
    col_mats = lax.dynamic_index_in_dim(col_ops, model, 0, keepdims=False)
    row_pass = jnp.einsum(
        "kij,jx->kix", row_mats, image, preferred_element_type=jnp.float32
    ).astype(jnp.bfloat16)
    return jnp.einsum("kix,kyx->iy", row_pass, col_mats, preferred_element_type=jnp.float32).astype(
        jnp.bfloat16
    )


def transpose_one(inputs, row_ops, col_ops):
    window, model = inputs
    row_mats = lax.dynamic_index_in_dim(row_ops, model, 0, keepdims=False)
    col_mats = lax.dynamic_index_in_dim(col_ops, model, 0, keepdims=False)
    back_pass = jnp.einsum(
        "iy,kyx->kix", window, col_mats, preferred_element_type=jnp.float32
    ).astype(jnp.bfloat16)
    return jnp.einsum(
        "kji,kjx->ix", row_mats, back_pass, preferred_element_type=jnp.float32
    ).astype(jnp.bfloat16)


def apply_all(function, images, models, row_ops, col_ops):
    bound = partial(function, row_ops=row_ops, col_ops=col_ops)
    return lax.map(bound, (images, models.astype(jnp.int32)), batch_size=32)


def per_device(stamps, tile_of, row_offset, col_offset, psf_model, psf_rows, psf_cols, cotangent):
    peer_count = lax.axis_size("tile")
    stamp_count, stamp_rows, stamp_cols = stamps.shape
    block_rows = stamp_rows // 2
    tile_rows, tile_cols = cotangent.shape
    row_blocks = tile_rows // block_rows
    col_blocks = tile_cols // stamp_cols
    capacity = max(2, (5 * stamp_count + 4 * peer_count - 1) // (4 * peer_count))
    slot_total = peer_count * capacity
    row_ops = build_ops(psf_rows, stamp_rows)
    col_ops = build_ops(psf_cols, stamp_cols)
    target = tile_of[:, 0]
    order = jnp.arange(stamp_count, dtype=jnp.int32)
    earlier = (target[None, :] == target[:, None]) & (order[None, :] < order[:, None])
    slots = target * capacity + jnp.sum(earlier.astype(jnp.int32), axis=1)
    slot_ids = jnp.arange(slot_total, dtype=jnp.int32)
    matches = slots[None, :] == slot_ids[:, None]
    place = matches.astype(jnp.bfloat16)
    details = jnp.stack([jnp.ones_like(target), row_offset, col_offset, psf_model], axis=1)
    detail_send = jnp.sum(jnp.where(matches[:, :, None], details[None, :, :], 0), axis=1)
    detail_send = detail_send.reshape(peer_count, capacity, 4)
    raw_send = jnp.dot(
        place,
        stamps.reshape((stamp_count, stamp_rows * stamp_cols)),
        preferred_element_type=jnp.float32,
    )
    raw_send = raw_send.astype(jnp.bfloat16).reshape(peer_count, capacity, stamp_rows, stamp_cols)
    raw_part = lax.all_to_all(raw_send, "tile", split_axis=0, concat_axis=0, tiled=True)
    info_part = lax.all_to_all(detail_send, "tile", split_axis=0, concat_axis=0, tiled=True)
    flat = raw_part.reshape((-1, stamp_rows, stamp_cols))
    result = apply_all(convolve_one, flat, info_part.reshape((-1, 4))[:, 3], row_ops, col_ops)
    received = result.reshape(raw_part.shape)
    info_flat = info_part.reshape((slot_total, 4))
    upper_block = info_flat[:, 1]
    block_ids = jnp.stack([upper_block, upper_block + 1], axis=1) * col_blocks + info_flat[:, 2:3]
    targets = jnp.arange((row_blocks + 1) * col_blocks, dtype=jnp.int32)
    placing = (block_ids.reshape(-1)[None, :] == targets[:, None]).astype(jnp.bfloat16)
    pieces = received.reshape((slot_total * 2, block_rows * stamp_cols))
    extended = jnp.dot(placing, pieces, preferred_element_type=jnp.float32)
    extended = extended.reshape(row_blocks + 1, col_blocks, block_rows, stamp_cols).transpose(
        0, 2, 1, 3
    )
    extended = extended.reshape((row_blocks + 1) * block_rows, tile_cols)
    arriving = passed_along(extended[tile_rows:].astype(jnp.bfloat16), "tile", 1).astype(
        jnp.float32
    )
    tile_sum = extended[:tile_rows].at[:block_rows].add(arriving)
    tile_image = tile_sum.astype(jnp.bfloat16)
    rim = passed_along(cotangent[:block_rows], "tile", -1)
    padded = jnp.concatenate([cotangent, rim], axis=0)
    blocks = padded.reshape(row_blocks + 1, block_rows, col_blocks, stamp_cols).transpose(
        0, 2, 1, 3
    )
    blocks = blocks.reshape((row_blocks + 1) * col_blocks, block_rows * stamp_cols)
    windows = lax.dot_general(
        placing, blocks, (((0,), (0,)), ((), ())), preferred_element_type=jnp.float32
    )
    windows = windows.astype(jnp.bfloat16).reshape(slot_total, stamp_rows, stamp_cols)
    slot_grads = apply_all(transpose_one, windows, info_flat[:, 3], row_ops, col_ops)
    slot_grads = slot_grads.reshape(peer_count, capacity, stamp_rows, stamp_cols)
    returned = lax.all_to_all(
        for_sending(slot_grads), "tile", split_axis=0, concat_axis=0, tiled=True
    ).astype(slot_grads.dtype)
    stamp_grad = lax.dot_general(
        place,
        returned.reshape((slot_total, stamp_rows * stamp_cols)),
        (((0,), (0,)), ((), ())),
        preferred_element_type=jnp.float32,
    )
    stamp_grad = stamp_grad.astype(jnp.bfloat16).reshape(stamp_count, stamp_rows, stamp_cols)
    return (tile_image, stamp_grad)


MESH = pl.DeviceIdType.MESH


def band_matrix(taps, lanes):
    count = taps.shape[1]
    half = (count - 1) // 2
    row = jnp.concatenate([taps, jnp.zeros((1, lanes - count), jnp.float32)], axis=1)
    spread = jnp.broadcast_to(row, (lanes, lanes))
    turned = pltpu.roll(spread, lanes - half, 1, stride=1, stride_axis=0)
    down = lax.broadcasted_iota(jnp.int32, (lanes, lanes), 0)
    across = lax.broadcasted_iota(jnp.int32, (lanes, lanes), 1)
    return jnp.where(jnp.abs(across - down) <= half, turned, 0.0)


def build_bands(taps_ref, row_fwd, row_bwd, col_fwd, col_bwd):
    models, terms = taps_ref.shape[0] // 2, taps_ref.shape[1]
    size = row_bwd.shape[1]
    lanes = col_bwd.shape[1]

    def build(m, carry):
        taps_rows, taps_cols = taps_ref[m], taps_ref[models + m]
        turned = []
        for k in range(terms):
            mat = band_matrix(taps_rows[k:k + 1], lanes)
            row_fwd[m, k * size:(k + 1) * size, :] = mat[:size, :size].astype(jnp.bfloat16)
            turned.append(mat.T[:size, :size].astype(jnp.bfloat16))
            mat = band_matrix(taps_cols[k:k + 1], lanes)
            col_bwd[m, :, k * lanes:(k + 1) * lanes] = mat.astype(jnp.bfloat16)
            col_fwd[m, k * lanes:(k + 1) * lanes, :] = mat.T.astype(jnp.bfloat16)
        row_bwd[m] = jnp.concatenate(turned, axis=1)
        return carry

    lax.fori_loop(0, models, build, 0)


def into_blocks(cot_ref, blocks_ref):
    block_count, block_rows, stamp_cols = blocks_ref.shape
    across = cot_ref.shape[1] // stamp_cols
    for b in range(block_count):
        top, left = b // across * block_rows, b % across * stamp_cols
        blocks_ref[b] = cot_ref[top:top + block_rows, left:left + stamp_cols]


def add_kernel(model_bits, col_blocks, group, codes, conv_ref, strip_ref, total):
    count, stamp_rows, stamp_cols = conv_ref.shape
    block_rows = stamp_rows // 2
    strip_rows = strip_ref.shape[0]

    def clear(i, carry):
        spot = pl.ds(pl.multiple_of(i * block_rows, block_rows), block_rows)
        total[spot, :] = jnp.zeros((block_rows, total.shape[1]), jnp.float32)
        return carry

    lax.fori_loop(0, total.shape[0] // block_rows, clear, 0)

    def some(g, carry):
        for u in range(group):
            block = codes[g * group + u] >> model_bits
            top = pl.multiple_of((block // col_blocks) * block_rows, block_rows)
            left = pl.multiple_of((block % col_blocks) * stamp_cols, stamp_cols)
            spot = (pl.ds(top, stamp_rows), pl.ds(left, stamp_cols))
            total[spot] = total[spot] + conv_ref[g * group + u].astype(jnp.float32)
        return carry

    lax.fori_loop(0, count // group, some, 0)

    def put(i, carry):
        spot = pl.ds(pl.multiple_of(i * block_rows, block_rows), block_rows)
        strip_ref[spot, :] = total[spot, :].astype(jnp.bfloat16)
        return carry

    lax.fori_loop(0, strip_rows // block_rows, put, 0)


class Place:
    def __init__(self, peers):
        self.planes = peers // 4
        self.me = lax.axis_index("tile")
        self.core = lax.rem(self.me, 2)
        self.row = lax.rem(self.me // 2, 2)
        self.plane = self.me // 4

    def at(self, shift=0, row=0, core=0):
        plane = lax.rem(self.plane + shift + self.planes, self.planes)
        y = 1 - self.row if row else self.row
        c = 1 - self.core if core else self.core
        return plane * 4 + y * 2 + c

    def greet(self):
        barrier = pltpu.get_barrier_semaphore()
        others = [self.at(d) for d in range(1, self.planes)] + [self.at(row=1), self.at(core=1)]
        for other in others:
            pl.semaphore_signal(barrier, inc=1, device_id={"tile": other}, device_id_type=MESH)
        pl.semaphore_wait(barrier, len(others))


def remote(src, dst, send, recv, device):
    return pltpu.make_async_remote_copy(src_ref=src, dst_ref=dst, send_sem=send, recv_sem=recv,
                                        device_id={"tile": device}, device_id_type=MESH)


def forward_kernel(peers, terms, model_bits, group, codes, taps_ref, stamps_hbm, pixels_ref,
                   conv_ref, sky, row_bwd, col_bwd, row_ops, col_ops, stamps_ref, cot_ref,
                   stamps_sem, own_sem, z_send, z_recv, y_send, y_recv, c_send, c_recv):
    place = Place(peers)
    planes = place.planes
    count, stamp_rows, stamp_cols = stamps_ref.shape
    groups = count // group

    def some(g, carry):
        for u in range(group):
            s = g * group + u
            model = codes[s] & ((1 << model_bits) - 1)
            first = jnp.dot(row_ops[model], stamps_ref[s],
                            preferred_element_type=jnp.float32).astype(jnp.bfloat16)
            wide = jnp.concatenate(
                [first[k * stamp_rows:(k + 1) * stamp_rows] for k in range(terms)], axis=1)
            conv_ref[s] = jnp.dot(wide, col_ops[model],
                                  preferred_element_type=jnp.float32).astype(jnp.bfloat16)
        return carry

    reached = [0]

    def compute(share):
        stop = min(groups, reached[0] + share)
        if stop > reached[0]:
            lax.fori_loop(reached[0], stop, some, 0)
        reached[0] = stop

    fetch = pltpu.make_async_copy(stamps_hbm, stamps_ref, stamps_sem)
    fetch.start()
    into_blocks(pixels_ref, cot_ref)
    sky[peers] = jnp.zeros(sky.shape[1:], jnp.bfloat16)
    place.greet()
    own = pltpu.make_async_copy(cot_ref, sky.at[place.me], own_sem)
    own.start()
    p = place.plane
    last = planes - 1

    def z_copy(tile, source, slot, step):
        return remote(source, sky.at[tile], z_send.at[slot], z_recv.at[slot], place.at(step))

    def y_copy(tile, source, slot):
        return remote(source, sky.at[tile], y_send.at[slot], y_recv.at[slot], place.at(row=1))

    def c_copy(tile, source, slot):
        return remote(source, sky.at[tile], c_send.at[slot], c_recv.at[slot], place.at(core=1))

    def streams(i, body):
        pl.when(p >= i)(lambda: body(-i, i, 1, p < last))
        pl.when(p + i <= last)(lambda: body(i, last + i, -1, p > 0))

    pl.when(p < last)(lambda: z_copy(place.me, cot_ref, 1, 1).start())
    pl.when(p > 0)(lambda: z_copy(place.me, cot_ref, last + 1, -1).start())
    y_copy(place.me, cot_ref, 0).start()
    c_copy(place.me, cot_ref, 0).start()
    build_bands(taps_ref, row_ops, row_bwd, col_ops, col_bwd)
    fetch.wait()
    compute(groups // 16)
    for i in range(1, planes):

        def arrived(shift, slot, step, more):
            tile = place.at(shift)
            source = sky.at[tile]
            z_copy(tile, source, slot, step).wait_recv()
            if i < last:
                pl.when(more)(lambda: z_copy(tile, source, slot + 1, step).start())
            y_copy(tile, source, slot).start()
            c_copy(tile, source, slot).start()

        streams(i, arrived)
        compute(groups * 4 // 16 if i < last else groups)

    half = 2 * last + 1

    def crossed(shift, slot):
        tile = place.at(shift, row=1)
        y_copy(tile, sky.at[tile], slot).wait_recv()
        c_copy(tile, sky.at[tile], half + slot).start()

    def finished(shift, slot):
        for row in range(2):
            tile = place.at(shift, row=row, core=1)
            c_copy(tile, sky.at[tile], row * half + slot).wait_recv()
            c_copy(tile, sky.at[tile], row * half + slot).wait_send()
        y_copy(tile, sky.at[tile], slot).wait_send()

    crossed(0, 0)
    for i in range(1, planes):
        streams(i, lambda shift, slot, step, more: crossed(shift, slot))
    finished(0, 0)
    own.wait()
    pl.when(p < last)(lambda: z_copy(place.me, cot_ref, 1, 1).wait_send())
    pl.when(p > 0)(lambda: z_copy(place.me, cot_ref, last + 1, -1).wait_send())
    for i in range(1, planes):

        def ended(shift, slot, step, more):
            finished(shift, slot)
            if i < last:
                tile = place.at(shift)
                pl.when(more)(lambda: z_copy(tile, sky.at[tile], slot + 1, step).wait_send())

        streams(i, ended)


def backward_kernel(peers, terms, model_bits, col_blocks, group, codes, row_ops, col_ops, sky,
                    strip, grads_ref, tile_ref, from_c, out_y, from_y, out_z, from_z,
                    z_send, z_recv, y_send, y_recv, c_send, c_recv):
    place = Place(peers)
    planes = place.planes
    count, stamp_rows, stamp_cols = grads_ref.shape
    groups = count // group
    block_rows = stamp_rows // 2
    tile_rows = tile_ref.shape[0]

    def some(g, carry):
        for u in range(group):
            s = g * group + u
            code = codes[s]
            model = code & ((1 << model_bits) - 1)
            block = code >> model_bits
            window = jnp.concatenate([sky[block], sky[block + col_blocks]], axis=0)
            first = jnp.dot(window, col_ops[model],
                            preferred_element_type=jnp.float32).astype(jnp.bfloat16)
            tall = jnp.concatenate(
                [first[:, k * stamp_cols:(k + 1) * stamp_cols] for k in range(terms)], axis=0)
            grads_ref[s] = jnp.dot(row_ops[model], tall,
                                   preferred_element_type=jnp.float32).astype(jnp.bfloat16)
        return carry

    reached = [0]

    def compute(share):
        stop = min(groups, reached[0] + share)
        if stop > reached[0]:
            lax.fori_loop(reached[0], stop, some, 0)
        reached[0] = stop

    def summed(store, *parts):
        def body(i, carry):
            spot = pl.ds(pl.multiple_of(i * block_rows, block_rows), block_rows)
            out = parts[0][0][parts[0][1], spot, :].astype(jnp.float32)
            for ref, index in parts[1:]:
                out = out + ref[index, spot, :].astype(jnp.float32)
            store(spot, out.astype(jnp.bfloat16))
            return carry

        lax.fori_loop(0, tile_rows // block_rows, body, 0)

    place.greet()
    p = place.plane
    last = planes - 1
    upper = p // 2
    mirrored = (1 - 2 * upper) * p + last * upper
    targets = [last * upper + (1 - 2 * upper) * q for q in (3, 2, 1 - mirrored, mirrored)]
    shifts = [q - p for q in targets]
    to_c, to_y = [], []
    for e in range(2 * planes):
        far = 1 if e < planes else 0
        source = strip.at[place.at(shifts[e % planes], row=far, core=1)]
        to_c.append(remote(source, from_c.at[e], c_send.at[e], c_recv.at[e], place.at(core=1)))
        to_c[-1].start()
    for i in range(planes):
        to_c[i].wait_recv()

        def keep(spot, value, i=i):
            out_y[i, spot, :] = value

        summed(keep, (strip, place.at(shifts[i], row=1)), (from_c, i))
        to_y.append(remote(out_y.at[i], from_y.at[i], y_send.at[i], y_recv.at[i], place.at(row=1)))
        to_y[-1].start()
    compute(groups * 4 // 16)

    def z_copy(i, slot, step):
        return remote(out_z.at[i], from_z.at[slot], z_send.at[i], z_recv.at[slot], place.at(step))

    for i in range(last):
        to_c[planes + i].wait_recv()
        to_y[i].wait_recv()
        target = targets[i]
        parts = [(strip, place.at(shifts[i])), (from_c, planes + i), (from_y, i)]

        def keep(spot, value):
            out_z[i, spot, :] = value

        def pass_on(slot, step, first):
            @pl.when(first)
            def _():
                summed(keep, *parts)

            @pl.when(jnp.logical_not(first))
            def _():
                z_copy(i, slot, step).wait_recv()
                summed(keep, *parts, (from_z, slot))

            z_copy(i, slot, step).start()

        pl.when(target > p)(lambda: pass_on(target, 1, p == 0))
        pl.when(target < p)(lambda: pass_on(planes + target, -1, p == last))
        compute(groups * 3 // 16)
    compute(groups)
    to_c[2 * planes - 1].wait_recv()
    to_y[last].wait_recv()
    parts = [(strip, place.me), (from_c, 2 * planes - 1), (from_y, last)]

    def finish(*slots):
        for slot in slots:
            z_copy(0, slot, 1).wait_recv()

        def keep(spot, value):
            tile_ref[spot, :] = value

        summed(keep, *parts, *[(from_z, slot) for slot in slots])

    pl.when(p == 0)(lambda: finish(planes + p))
    pl.when(p == last)(lambda: finish(p))
    pl.when(jnp.logical_and(p > 0, p < last))(lambda: finish(p, planes + p))
    for copy in to_c + to_y:
        copy.wait_send()
    for i in range(last):
        z_copy(i, i, 1).wait_send()


def divisor(number, wanted):
    return max(d for d in range(1, wanted + 1) if number % d == 0)


def in_place(stamps, tile_of, row_offset, col_offset, psf_model, psf_rows, psf_cols, cotangent):
    peers = lax.axis_size("tile")
    planes = peers // 4
    stamp_count, stamp_rows, stamp_cols = stamps.shape
    models, terms, taps = psf_rows.shape
    block_rows = stamp_rows // 2
    tile_rows, tile_cols = cotangent.shape
    row_blocks = tile_rows // block_rows
    col_blocks = tile_cols // stamp_cols
    strip_rows = peers * tile_rows
    model_bits = max(1, (models - 1).bit_length())
    upper = tile_of[:, 0] * row_blocks + row_offset
    codes = ((upper * col_blocks + col_offset) << model_bits) + psf_model
    group = divisor(stamp_count, 8)
    flops = 2 * stamp_count * terms * stamp_rows * stamp_cols * (stamp_rows + stamp_cols)
    cost = pl.CostEstimate(flops=8 * flops, bytes_accessed=40 << 20, transcendentals=0)
    smem = pl.BlockSpec(memory_space=pltpu.SMEM)
    vmem = pl.BlockSpec(memory_space=pltpu.VMEM)
    anywhere = pl.BlockSpec(memory_space=pl.ANY)
    short = jnp.bfloat16
    dma = pltpu.SemaphoreType.DMA
    limit = 44 << 20
    block_shape = (row_blocks * col_blocks, block_rows, stamp_cols)

    conv, sky, row_bwd, col_bwd = pl.pallas_call(
        partial(forward_kernel, peers, terms, model_bits, group),
        out_shape=(
            jax.ShapeDtypeStruct(stamps.shape, short),
            jax.ShapeDtypeStruct((peers + 1,) + block_shape, short),
            jax.ShapeDtypeStruct((models, stamp_rows, terms * stamp_rows), short),
            jax.ShapeDtypeStruct((models, stamp_cols, terms * stamp_cols), short),
        ),
        in_specs=[smem, vmem, anywhere, vmem],
        out_specs=(vmem,) * 4,
        scratch_shapes=[
            pltpu.VMEM((models, terms * stamp_rows, stamp_rows), short),
            pltpu.VMEM((models, terms * stamp_cols, stamp_cols), short),
            pltpu.VMEM(stamps.shape, short),
            pltpu.VMEM(block_shape, short),
        ] + [dma, dma] + [dma((2 * planes - 1,))] * 4 + [dma((4 * planes - 2,))] * 2,
        compiler_params=pltpu.CompilerParams(collective_id=0, has_side_effects=True,
                                             vmem_limit_bytes=limit),
        cost_estimate=cost,
    )(codes, jnp.concatenate([psf_rows, psf_cols], axis=0), stamps, cotangent)
    strip = pl.pallas_call(
        partial(add_kernel, model_bits, col_blocks, group),
        out_shape=jax.ShapeDtypeStruct((strip_rows, tile_cols), short),
        in_specs=[smem, vmem],
        out_specs=vmem,
        scratch_shapes=[pltpu.VMEM((strip_rows + block_rows, tile_cols), jnp.float32)],
        compiler_params=pltpu.CompilerParams(vmem_limit_bytes=limit),
    )(codes, conv)
    tile = (tile_rows, tile_cols)
    stamp_grad, tile_image = pl.pallas_call(
        partial(backward_kernel, peers, terms, model_bits, col_blocks, group),
        out_shape=(
            jax.ShapeDtypeStruct(stamps.shape, short),
            jax.ShapeDtypeStruct(tile, short),
        ),
        in_specs=[smem, vmem, vmem, vmem, vmem],
        out_specs=(vmem, vmem),
        scratch_shapes=[
            pltpu.VMEM((2 * planes,) + tile, short),
            pltpu.VMEM((planes,) + tile, short),
            pltpu.VMEM((planes,) + tile, short),
            pltpu.VMEM((planes,) + tile, short),
            pltpu.VMEM((2 * planes,) + tile, short),
            dma((planes,)), dma((2 * planes,)), dma((planes,)), dma((planes,)),
            dma((2 * planes,)), dma((2 * planes,)),
        ],
        compiler_params=pltpu.CompilerParams(collective_id=1, has_side_effects=True,
                                             vmem_limit_bytes=limit),
        cost_estimate=cost,
    )(codes, row_bwd, col_bwd, sky.reshape((-1,) + block_shape[1:]),
      strip.reshape((peers,) + tile))
    return tile_image, stamp_grad


def strip_fits(peers, cotangent):
    rows, cols = cotangent.shape
    return peers == 16 and peers * rows * cols * 4 <= 12 << 20


def per_device_any(*args):
    if strip_fits(lax.axis_size("tile"), args[-1]):
        return in_place(*args)
    return per_device(*args)


def solution(mesh):
    in_specs = (
        P(("band", "tile"), None, None),
        P(("band", "tile"), None),
        P(("band", "tile")),
        P(("band", "tile")),
        P(("band", "tile")),
        P("band", None, None),
        P("band", None, None),
        P(("band", "tile"), None),
    )
    out_specs = (P(("band", "tile"), None), P(("band", "tile"), None, None))
    return jax.shard_map(
        per_device_any, mesh=mesh, in_specs=in_specs, out_specs=out_specs, check_vma=False
    )
```

```python
from functools import partial

import jax
import jax.numpy as jnp
from jax import lax
from jax.experimental import pallas as pl
from jax.experimental.pallas import tpu as pltpu
from jax.sharding import PartitionSpec as P


def passed_along(array, axis, by):
    peers = lax.axis_size(axis)
    pairs = [(i, i + by) for i in range(peers) if 0 <= i + by < peers]
    return lax.ppermute(array, axis, pairs)


def for_sending(array):

    def short(part):
        return part.astype(jnp.bfloat16) if part.dtype == jnp.float32 else part

    return jax.tree.map(short, array)


def band_table(taps_count, size):
    half_width = (taps_count - 1) // 2
    places = jnp.arange(size, dtype=jnp.int32)
    offsets = places[None, :] - places[:, None] + half_width
    taps_index = jnp.arange(taps_count, dtype=jnp.int32)
    table = (offsets[None, :, :] == taps_index[:, None, None]).astype(jnp.float32)
    return table.reshape((taps_count, size * size))


def build_ops(profiles, size):
    model_total, term_total, taps_count = profiles.shape
    table = band_table(taps_count, size)
    mats = jnp.dot(
        profiles.reshape((model_total * term_total, taps_count)),
        table,
        precision=lax.Precision.HIGHEST,
    )
    return mats.reshape((model_total, term_total, size, size)).astype(jnp.bfloat16)


def convolve_one(inputs, row_ops, col_ops):
    image, model = inputs
    row_mats = lax.dynamic_index_in_dim(row_ops, model, 0, keepdims=False)
    col_mats = lax.dynamic_index_in_dim(col_ops, model, 0, keepdims=False)
    row_pass = jnp.einsum(
        "kij,jx->kix", row_mats, image, preferred_element_type=jnp.float32
    ).astype(jnp.bfloat16)
    return jnp.einsum("kix,kyx->iy", row_pass, col_mats, preferred_element_type=jnp.float32).astype(
        jnp.bfloat16
    )


def transpose_one(inputs, row_ops, col_ops):
    window, model = inputs
    row_mats = lax.dynamic_index_in_dim(row_ops, model, 0, keepdims=False)
    col_mats = lax.dynamic_index_in_dim(col_ops, model, 0, keepdims=False)
    back_pass = jnp.einsum(
        "iy,kyx->kix", window, col_mats, preferred_element_type=jnp.float32
    ).astype(jnp.bfloat16)
    return jnp.einsum(
        "kji,kjx->ix", row_mats, back_pass, preferred_element_type=jnp.float32
    ).astype(jnp.bfloat16)


def apply_all(function, images, models, row_ops, col_ops):
    bound = partial(function, row_ops=row_ops, col_ops=col_ops)
    return lax.map(bound, (images, models.astype(jnp.int32)), batch_size=32)


def per_device(stamps, tile_of, row_offset, col_offset, psf_model, psf_rows, psf_cols, cotangent):
    peer_count = lax.axis_size("tile")
    stamp_count, stamp_rows, stamp_cols = stamps.shape
    block_rows = stamp_rows // 2
    tile_rows, tile_cols = cotangent.shape
    row_blocks = tile_rows // block_rows
    col_blocks = tile_cols // stamp_cols
    capacity = max(2, (5 * stamp_count + 4 * peer_count - 1) // (4 * peer_count))
    slot_total = peer_count * capacity
    row_ops = build_ops(psf_rows, stamp_rows)
    col_ops = build_ops(psf_cols, stamp_cols)
    target = tile_of[:, 0]
    order = jnp.arange(stamp_count, dtype=jnp.int32)
    earlier = (target[None, :] == target[:, None]) & (order[None, :] < order[:, None])
    slots = target * capacity + jnp.sum(earlier.astype(jnp.int32), axis=1)
    slot_ids = jnp.arange(slot_total, dtype=jnp.int32)
    matches = slots[None, :] == slot_ids[:, None]
    place = matches.astype(jnp.bfloat16)
    details = jnp.stack([jnp.ones_like(target), row_offset, col_offset, psf_model], axis=1)
    detail_send = jnp.sum(jnp.where(matches[:, :, None], details[None, :, :], 0), axis=1)
    detail_send = detail_send.reshape(peer_count, capacity, 4)
    raw_send = jnp.dot(
        place,
        stamps.reshape((stamp_count, stamp_rows * stamp_cols)),
        preferred_element_type=jnp.float32,
    )
    raw_send = raw_send.astype(jnp.bfloat16).reshape(peer_count, capacity, stamp_rows, stamp_cols)
    raw_part = lax.all_to_all(raw_send, "tile", split_axis=0, concat_axis=0, tiled=True)
    info_part = lax.all_to_all(detail_send, "tile", split_axis=0, concat_axis=0, tiled=True)
    flat = raw_part.reshape((-1, stamp_rows, stamp_cols))
    result = apply_all(convolve_one, flat, info_part.reshape((-1, 4))[:, 3], row_ops, col_ops)
    received = result.reshape(raw_part.shape)
    info_flat = info_part.reshape((slot_total, 4))
    upper_block = info_flat[:, 1]
    block_ids = jnp.stack([upper_block, upper_block + 1], axis=1) * col_blocks + info_flat[:, 2:3]
    targets = jnp.arange((row_blocks + 1) * col_blocks, dtype=jnp.int32)
    placing = (block_ids.reshape(-1)[None, :] == targets[:, None]).astype(jnp.bfloat16)
    pieces = received.reshape((slot_total * 2, block_rows * stamp_cols))
    extended = jnp.dot(placing, pieces, preferred_element_type=jnp.float32)
    extended = extended.reshape(row_blocks + 1, col_blocks, block_rows, stamp_cols).transpose(
        0, 2, 1, 3
    )
    extended = extended.reshape((row_blocks + 1) * block_rows, tile_cols)
    arriving = passed_along(extended[tile_rows:].astype(jnp.bfloat16), "tile", 1).astype(
        jnp.float32
    )
    tile_sum = extended[:tile_rows].at[:block_rows].add(arriving)
    tile_image = tile_sum.astype(jnp.bfloat16)
    rim = passed_along(cotangent[:block_rows], "tile", -1)
    padded = jnp.concatenate([cotangent, rim], axis=0)
    blocks = padded.reshape(row_blocks + 1, block_rows, col_blocks, stamp_cols).transpose(
        0, 2, 1, 3
    )
    blocks = blocks.reshape((row_blocks + 1) * col_blocks, block_rows * stamp_cols)
    windows = lax.dot_general(
        placing, blocks, (((0,), (0,)), ((), ())), preferred_element_type=jnp.float32
    )
    windows = windows.astype(jnp.bfloat16).reshape(slot_total, stamp_rows, stamp_cols)
    slot_grads = apply_all(transpose_one, windows, info_flat[:, 3], row_ops, col_ops)
    slot_grads = slot_grads.reshape(peer_count, capacity, stamp_rows, stamp_cols)
    returned = lax.all_to_all(
        for_sending(slot_grads), "tile", split_axis=0, concat_axis=0, tiled=True
    ).astype(slot_grads.dtype)
    stamp_grad = lax.dot_general(
        place,
        returned.reshape((slot_total, stamp_rows * stamp_cols)),
        (((0,), (0,)), ((), ())),
        preferred_element_type=jnp.float32,
    )
    stamp_grad = stamp_grad.astype(jnp.bfloat16).reshape(stamp_count, stamp_rows, stamp_cols)
    return (tile_image, stamp_grad)


MESH = pl.DeviceIdType.MESH


def band_matrix(taps, lanes):
    count = taps.shape[1]
    half = (count - 1) // 2
    row = jnp.concatenate([taps, jnp.zeros((1, lanes - count), jnp.float32)], axis=1)
    spread = jnp.broadcast_to(row, (lanes, lanes))
    turned = pltpu.roll(spread, lanes - half, 1, stride=1, stride_axis=0)
    down = lax.broadcasted_iota(jnp.int32, (lanes, lanes), 0)
    across = lax.broadcasted_iota(jnp.int32, (lanes, lanes), 1)
    return jnp.where(jnp.abs(across - down) <= half, turned, 0.0)


def build_bands(taps_ref, row_fwd, row_bwd, col_fwd, col_bwd):
    models, terms = taps_ref.shape[0] // 2, taps_ref.shape[1]
    size = row_bwd.shape[1]
    lanes = col_bwd.shape[1]

    def build(m, carry):
        taps_rows, taps_cols = taps_ref[m], taps_ref[models + m]
        turned = []
        for k in range(terms):
            mat = band_matrix(taps_rows[k:k + 1], lanes)
            row_fwd[m, k * size:(k + 1) * size, :] = mat[:size, :size].astype(jnp.bfloat16)
            turned.append(mat.T[:size, :size].astype(jnp.bfloat16))
            mat = band_matrix(taps_cols[k:k + 1], lanes)
            col_bwd[m, :, k * lanes:(k + 1) * lanes] = mat.astype(jnp.bfloat16)
            col_fwd[m, k * lanes:(k + 1) * lanes, :] = mat.T.astype(jnp.bfloat16)
        row_bwd[m] = jnp.concatenate(turned, axis=1)
        return carry

    lax.fori_loop(0, models, build, 0)


def into_blocks(cot_ref, blocks_ref):
    block_count, block_rows, stamp_cols = blocks_ref.shape
    across = cot_ref.shape[1] // stamp_cols
    for b in range(block_count):
        top, left = b // across * block_rows, b % across * stamp_cols
        blocks_ref[b] = cot_ref[top:top + block_rows, left:left + stamp_cols]


def add_kernel(model_bits, col_blocks, group, codes, conv_ref, strip_ref, total):
    count, stamp_rows, stamp_cols = conv_ref.shape
    block_rows = stamp_rows // 2
    strip_rows = strip_ref.shape[0]

    def clear(i, carry):
        spot = pl.ds(pl.multiple_of(i * block_rows, block_rows), block_rows)
        total[spot, :] = jnp.zeros((block_rows, total.shape[1]), jnp.float32)
        return carry

    lax.fori_loop(0, total.shape[0] // block_rows, clear, 0)

    def some(g, carry):
        for u in range(group):
            block = codes[g * group + u] >> model_bits
            top = pl.multiple_of((block // col_blocks) * block_rows, block_rows)
            left = pl.multiple_of((block % col_blocks) * stamp_cols, stamp_cols)
            spot = (pl.ds(top, stamp_rows), pl.ds(left, stamp_cols))
            total[spot] = total[spot] + conv_ref[g * group + u].astype(jnp.float32)
        return carry

    lax.fori_loop(0, count // group, some, 0)

    def put(i, carry):
        spot = pl.ds(pl.multiple_of(i * block_rows, block_rows), block_rows)
        strip_ref[spot, :] = total[spot, :].astype(jnp.bfloat16)
        return carry

    lax.fori_loop(0, strip_rows // block_rows, put, 0)


class Place:
    def __init__(self, peers):
        self.planes = peers // 4
        self.me = lax.axis_index("tile")
        self.core = lax.rem(self.me, 2)
        self.row = lax.rem(self.me // 2, 2)
        self.plane = self.me // 4

    def at(self, shift=0, row=0, core=0):
        plane = lax.rem(self.plane + shift + self.planes, self.planes)
        y = 1 - self.row if row else self.row
        c = 1 - self.core if core else self.core
        return plane * 4 + y * 2 + c

    def greet(self):
        barrier = pltpu.get_barrier_semaphore()
        others = [self.at(d) for d in range(1, self.planes)] + [self.at(row=1), self.at(core=1)]
        for other in others:
            pl.semaphore_signal(barrier, inc=1, device_id={"tile": other}, device_id_type=MESH)
        pl.semaphore_wait(barrier, len(others))


def remote(src, dst, send, recv, device):
    return pltpu.make_async_remote_copy(src_ref=src, dst_ref=dst, send_sem=send, recv_sem=recv,
                                        device_id={"tile": device}, device_id_type=MESH)


def forward_kernel(peers, terms, model_bits, group, codes, taps_ref, stamps_hbm, pixels_ref,
                   conv_ref, sky, row_bwd, col_bwd, row_ops, col_ops, stamps_ref, cot_ref,
                   stamps_sem, own_sem, z_send, z_recv, y_send, y_recv, c_send, c_recv):
    place = Place(peers)
    planes = place.planes
    count, stamp_rows, stamp_cols = stamps_ref.shape
    groups = count // group

    def some(g, carry):
        for u in range(group):
            s = g * group + u
            model = codes[s] & ((1 << model_bits) - 1)
            first = jnp.dot(row_ops[model], stamps_ref[s],
                            preferred_element_type=jnp.float32).astype(jnp.bfloat16)
            wide = jnp.concatenate(
                [first[k * stamp_rows:(k + 1) * stamp_rows] for k in range(terms)], axis=1)
            conv_ref[s] = jnp.dot(wide, col_ops[model],
                                  preferred_element_type=jnp.float32).astype(jnp.bfloat16)
        return carry

    reached = [0]

    def compute(share):
        stop = min(groups, reached[0] + share)
        if stop > reached[0]:
            lax.fori_loop(reached[0], stop, some, 0)
        reached[0] = stop

    fetch = pltpu.make_async_copy(stamps_hbm, stamps_ref, stamps_sem)
    fetch.start()
    into_blocks(pixels_ref, cot_ref)
    sky[peers] = jnp.zeros(sky.shape[1:], jnp.bfloat16)
    place.greet()
    own = pltpu.make_async_copy(cot_ref, sky.at[place.me], own_sem)
    own.start()
    p = place.plane
    last = planes - 1

    def z_copy(tile, source, slot, step):
        return remote(source, sky.at[tile], z_send.at[slot], z_recv.at[slot], place.at(step))

    def y_copy(tile, source, slot):
        return remote(source, sky.at[tile], y_send.at[slot], y_recv.at[slot], place.at(row=1))

    def c_copy(tile, source, slot):
        return remote(source, sky.at[tile], c_send.at[slot], c_recv.at[slot], place.at(core=1))

    def streams(i, body):
        pl.when(p >= i)(lambda: body(-i, i, 1, p < last))
        pl.when(p + i <= last)(lambda: body(i, last + i, -1, p > 0))

    y_copy(place.me, cot_ref, 0).start()
    pl.when(p < last)(lambda: z_copy(place.me, cot_ref, 1, 1).start())
    pl.when(p > 0)(lambda: z_copy(place.me, cot_ref, last + 1, -1).start())
    c_copy(place.me, cot_ref, 0).start()
    build_bands(taps_ref, row_ops, row_bwd, col_ops, col_bwd)
    fetch.wait()
    compute(groups // 16)
    for i in range(1, planes):

        def arrived(shift, slot, step, more):
            tile = place.at(shift)
            source = sky.at[tile]
            z_copy(tile, source, slot, step).wait_recv()
            if i < last:
                pl.when(more)(lambda: z_copy(tile, source, slot + 1, step).start())
            y_copy(tile, source, slot).start()
            c_copy(tile, source, slot).start()

        streams(i, arrived)
        compute(groups * 3 // 16 if i < last else groups)

    half = 2 * last + 1

    def crossed(shift, slot):
        tile = place.at(shift, row=1)
        y_copy(tile, sky.at[tile], slot).wait_recv()
        c_copy(tile, sky.at[tile], half + slot).start()

    def finished(shift, slot):
        for row in range(2):
            tile = place.at(shift, row=row, core=1)
            c_copy(tile, sky.at[tile], row * half + slot).wait_recv()
            c_copy(tile, sky.at[tile], row * half + slot).wait_send()
        y_copy(tile, sky.at[tile], slot).wait_send()

    crossed(0, 0)
    for i in range(1, planes):
        streams(i, lambda shift, slot, step, more: crossed(shift, slot))
    finished(0, 0)
    own.wait()
    pl.when(p < last)(lambda: z_copy(place.me, cot_ref, 1, 1).wait_send())
    pl.when(p > 0)(lambda: z_copy(place.me, cot_ref, last + 1, -1).wait_send())
    for i in range(1, planes):

        def ended(shift, slot, step, more):
            finished(shift, slot)
            if i < last:
                tile = place.at(shift)
                pl.when(more)(lambda: z_copy(tile, sky.at[tile], slot + 1, step).wait_send())

        streams(i, ended)


def backward_kernel(peers, terms, model_bits, col_blocks, group, codes, row_ops, col_ops, sky,
                    strip, grads_ref, tile_ref, from_c, out_y, from_y, out_z, from_z,
                    z_send, z_recv, y_send, y_recv, c_send, c_recv):
    place = Place(peers)
    planes = place.planes
    count, stamp_rows, stamp_cols = grads_ref.shape
    groups = count // group
    block_rows = stamp_rows // 2
    tile_rows = tile_ref.shape[0]

    def some(g, carry):
        for u in range(group):
            s = g * group + u
            code = codes[s]
            model = code & ((1 << model_bits) - 1)
            block = code >> model_bits
            window = jnp.concatenate([sky[block], sky[block + col_blocks]], axis=0)
            first = jnp.dot(window, col_ops[model],
                            preferred_element_type=jnp.float32).astype(jnp.bfloat16)
            tall = jnp.concatenate(
                [first[:, k * stamp_cols:(k + 1) * stamp_cols] for k in range(terms)], axis=0)
            grads_ref[s] = jnp.dot(row_ops[model], tall,
                                   preferred_element_type=jnp.float32).astype(jnp.bfloat16)
        return carry

    reached = [0]

    def compute(share):
        stop = min(groups, reached[0] + share)
        if stop > reached[0]:
            lax.fori_loop(reached[0], stop, some, 0)
        reached[0] = stop

    def summed(store, *parts):
        def body(i, carry):
            spot = pl.ds(pl.multiple_of(i * block_rows, block_rows), block_rows)
            out = parts[0][0][parts[0][1], spot, :].astype(jnp.float32)
            for ref, index in parts[1:]:
                out = out + ref[index, spot, :].astype(jnp.float32)
            store(spot, out.astype(jnp.bfloat16))
            return carry

        lax.fori_loop(0, tile_rows // block_rows, body, 0)

    place.greet()
    p = place.plane
    last = planes - 1
    upper = p // 2
    mirrored = (1 - 2 * upper) * p + last * upper
    targets = [last * upper + (1 - 2 * upper) * q for q in (3, 2, 1 - mirrored, mirrored)]
    shifts = [q - p for q in targets]
    to_c, to_y = [], []
    for e in range(2 * planes):
        far = 1 if e < planes else 0
        source = strip.at[place.at(shifts[e % planes], row=far, core=1)]
        to_c.append(remote(source, from_c.at[e], c_send.at[e], c_recv.at[e], place.at(core=1)))
        to_c[-1].start()
    for i in range(planes):
        to_c[i].wait_recv()

        def keep(spot, value, i=i):
            out_y[i, spot, :] = value

        summed(keep, (strip, place.at(shifts[i], row=1)), (from_c, i))
        to_y.append(remote(out_y.at[i], from_y.at[i], y_send.at[i], y_recv.at[i], place.at(row=1)))
        to_y[-1].start()
    compute(groups * 4 // 16)

    def z_copy(i, slot, step):
        return remote(out_z.at[i], from_z.at[slot], z_send.at[i], z_recv.at[slot], place.at(step))

    for i in range(last):
        to_c[planes + i].wait_recv()
        to_y[i].wait_recv()
        target = targets[i]
        parts = [(strip, place.at(shifts[i])), (from_c, planes + i), (from_y, i)]

        def keep(spot, value):
            out_z[i, spot, :] = value

        def pass_on(slot, step, first):
            @pl.when(first)
            def _():
                summed(keep, *parts)

            @pl.when(jnp.logical_not(first))
            def _():
                z_copy(i, slot, step).wait_recv()
                summed(keep, *parts, (from_z, slot))

            z_copy(i, slot, step).start()

        pl.when(target > p)(lambda: pass_on(target, 1, p == 0))
        pl.when(target < p)(lambda: pass_on(planes + target, -1, p == last))
        compute(groups * 3 // 16)
    compute(groups)
    to_c[2 * planes - 1].wait_recv()
    to_y[last].wait_recv()
    parts = [(strip, place.me), (from_c, 2 * planes - 1), (from_y, last)]

    def finish(*slots):
        for slot in slots:
            z_copy(0, slot, 1).wait_recv()

        def keep(spot, value):
            tile_ref[spot, :] = value

        summed(keep, *parts, *[(from_z, slot) for slot in slots])

    pl.when(p == 0)(lambda: finish(planes + p))
    pl.when(p == last)(lambda: finish(p))
    pl.when(jnp.logical_and(p > 0, p < last))(lambda: finish(p, planes + p))
    for copy in to_c + to_y:
        copy.wait_send()
    for i in range(last):
        z_copy(i, i, 1).wait_send()


def divisor(number, wanted):
    return max(d for d in range(1, wanted + 1) if number % d == 0)


def in_place(stamps, tile_of, row_offset, col_offset, psf_model, psf_rows, psf_cols, cotangent):
    peers = lax.axis_size("tile")
    planes = peers // 4
    stamp_count, stamp_rows, stamp_cols = stamps.shape
    models, terms, taps = psf_rows.shape
    block_rows = stamp_rows // 2
    tile_rows, tile_cols = cotangent.shape
    row_blocks = tile_rows // block_rows
    col_blocks = tile_cols // stamp_cols
    strip_rows = peers * tile_rows
    model_bits = max(1, (models - 1).bit_length())
    upper = tile_of[:, 0] * row_blocks + row_offset
    codes = ((upper * col_blocks + col_offset) << model_bits) + psf_model
    group = divisor(stamp_count, 8)
    flops = 2 * stamp_count * terms * stamp_rows * stamp_cols * (stamp_rows + stamp_cols)
    cost = pl.CostEstimate(flops=8 * flops, bytes_accessed=40 << 20, transcendentals=0)
    smem = pl.BlockSpec(memory_space=pltpu.SMEM)
    vmem = pl.BlockSpec(memory_space=pltpu.VMEM)
    anywhere = pl.BlockSpec(memory_space=pl.ANY)
    short = jnp.bfloat16
    dma = pltpu.SemaphoreType.DMA
    limit = 44 << 20
    block_shape = (row_blocks * col_blocks, block_rows, stamp_cols)

    conv, sky, row_bwd, col_bwd = pl.pallas_call(
        partial(forward_kernel, peers, terms, model_bits, group),
        out_shape=(
            jax.ShapeDtypeStruct(stamps.shape, short),
            jax.ShapeDtypeStruct((peers + 1,) + block_shape, short),
            jax.ShapeDtypeStruct((models, stamp_rows, terms * stamp_rows), short),
            jax.ShapeDtypeStruct((models, stamp_cols, terms * stamp_cols), short),
        ),
        in_specs=[smem, vmem, anywhere, vmem],
        out_specs=(vmem,) * 4,
        scratch_shapes=[
            pltpu.VMEM((models, terms * stamp_rows, stamp_rows), short),
            pltpu.VMEM((models, terms * stamp_cols, stamp_cols), short),
            pltpu.VMEM(stamps.shape, short),
            pltpu.VMEM(block_shape, short),
        ] + [dma, dma] + [dma((2 * planes - 1,))] * 4 + [dma((4 * planes - 2,))] * 2,
        compiler_params=pltpu.CompilerParams(collective_id=0, has_side_effects=True,
                                             vmem_limit_bytes=limit),
        cost_estimate=cost,
    )(codes, jnp.concatenate([psf_rows, psf_cols], axis=0), stamps, cotangent)
    strip = pl.pallas_call(
        partial(add_kernel, model_bits, col_blocks, group),
        out_shape=jax.ShapeDtypeStruct((strip_rows, tile_cols), short),
        in_specs=[smem, vmem],
        out_specs=vmem,
        scratch_shapes=[pltpu.VMEM((strip_rows + block_rows, tile_cols), jnp.float32)],
        compiler_params=pltpu.CompilerParams(vmem_limit_bytes=limit),
    )(codes, conv)
    tile = (tile_rows, tile_cols)
    stamp_grad, tile_image = pl.pallas_call(
        partial(backward_kernel, peers, terms, model_bits, col_blocks, group),
        out_shape=(
            jax.ShapeDtypeStruct(stamps.shape, short),
            jax.ShapeDtypeStruct(tile, short),
        ),
        in_specs=[smem, vmem, vmem, vmem, vmem],
        out_specs=(vmem, vmem),
        scratch_shapes=[
            pltpu.VMEM((2 * planes,) + tile, short),
            pltpu.VMEM((planes,) + tile, short),
            pltpu.VMEM((planes,) + tile, short),
            pltpu.VMEM((planes,) + tile, short),
            pltpu.VMEM((2 * planes,) + tile, short),
            dma((planes,)), dma((2 * planes,)), dma((planes,)), dma((planes,)),
            dma((2 * planes,)), dma((2 * planes,)),
        ],
        compiler_params=pltpu.CompilerParams(collective_id=1, has_side_effects=True,
                                             vmem_limit_bytes=limit),
        cost_estimate=cost,
    )(codes, row_bwd, col_bwd, sky.reshape((-1,) + block_shape[1:]),
      strip.reshape((peers,) + tile))
    return tile_image, stamp_grad


def strip_fits(peers, cotangent):
    rows, cols = cotangent.shape
    return peers == 16 and peers * rows * cols * 4 <= 12 << 20


def per_device_any(*args):
    if strip_fits(lax.axis_size("tile"), args[-1]):
        return in_place(*args)
    return per_device(*args)


def solution(mesh):
    in_specs = (
        P(("band", "tile"), None, None),
        P(("band", "tile"), None),
        P(("band", "tile")),
        P(("band", "tile")),
        P(("band", "tile")),
        P("band", None, None),
        P("band", None, None),
        P(("band", "tile"), None),
    )
    out_specs = (P(("band", "tile"), None), P(("band", "tile"), None, None))
    return jax.shard_map(
        per_device_any, mesh=mesh, in_specs=in_specs, out_specs=out_specs, check_vma=False
    )
```
